128 devices in a mesh: pb: 8 (over z_hi, y), ka: 16 (over z_lo, x, core).
Axes of the slice: x: 4, y: 4, z: 4 (z_hi: 2, z_lo: 2; z = z_hi * 2 + z_lo), core: 2. Of those that a mesh axis runs over, the one named last changes fastest.
Arguments:
- queries: bfloat16 [4096, 1024], P(('pb', 'ka')), may hold values from -6 to 6
- d_out: bfloat16 [4096, 1024], P(('pb', 'ka')), may hold values from -6 to 6
- log_sums: float32 [8, 4096], P(None, ('pb', 'ka')), as said below
- deltas: float32 [8, 4096], P(None, ('pb', 'ka')), may hold values from -4 to 4
- query_start: int32 [32], P('pb'), may hold values from 0 to 32640, as said below
- key_codes: bfloat16 [32768, 128], P(('ka', 'pb')), may hold values from -127 to 127, as said below
- value_codes: bfloat16 [32768, 128], P(('ka', 'pb')), may hold values from -127 to 127, as said below
- key_scale: float32 [32768], P(('ka', 'pb')), may hold values from 0.002 to 0.02
- value_scale: float32 [32768], P(('ka', 'pb')), may hold values from 0.002 to 0.02
- key_start: int32 [256], P('ka'), may hold values from 0 to 32640, as said below
Outputs:
- grad_queries: bfloat16 [4096, 1024], P(('pb', 'ka'))
- grad_keys: bfloat16 [32768, 128], P(('ka', 'pb'))
- grad_values: bfloat16 [32768, 128], P(('ka', 'pb'))
The draws below stay inside these ranges and needn't reach their ends.
Inputs may be any that keep to these rules, and one draw needn't show every extreme that they name: `query_start`: distinct multiples of 128, and 32640 is one of them. `key_start`: each multiple of 128 below 32768 exactly once, so that the keys cover positions 0 to 32767. `key_codes`: whole numbers. `value_codes`: whole numbers. log_sums[h, i] - log(1 + p) lies between 0.5 and 3, where p is query i's position.
All inputs are finite; a program needn't handle non-finite values.
Results may differ from the reference program's by a relative error of at most 0.012.
The reference program's roundings to bfloat16 on the way (of `key_rows`, `value_rows`, `attention_low` and `dscores`) count: a program that leaves them out, or rounds other values in their place, can miss the bound.
Values may be sent and summed in bfloat16 or wider, within the bound.
A program may use at most 64 MiB of HBM per device.

```python
import math
import jax
import jax.numpy as jnp
from jax import lax

HEADS = 8
HEAD_DIM = 128
BLOCK = 128
KTILE = 2048
SQ = 4096
SK = 32768
N_KA = 16


def block_starts(key):
    total_blocks = SK // BLOCK
    query_blocks = SQ // BLOCK
    base = jax.random.fold_in(key, 7)
    key_order = jax.random.permutation(jax.random.fold_in(base, 1), total_blocks)
    chosen = jax.random.permutation(jax.random.fold_in(base, 2), total_blocks - 1)[:query_blocks - 1]
    blocks = jnp.concatenate([chosen.astype(jnp.int32), jnp.full((1,), total_blocks - 1, jnp.int32)])
    query_order = jax.random.permutation(jax.random.fold_in(base, 3), query_blocks)
    query_first = (blocks[query_order] * BLOCK).astype(jnp.int32)
    key_first = (key_order * BLOCK).astype(jnp.int32)
    return (query_first, key_first)


def draw_query_start(key, part):
    return block_starts(key)[0]


def draw_key_start(key, part):
    return block_starts(key)[1]


def draw_log_sums(key, part):
    query_first = block_starts(key)[0]
    offsets = jnp.arange(BLOCK, dtype=jnp.int32)
    position = (query_first[:, None] + offsets[None, :]).reshape(-1).astype(jnp.float32)
    margin = jax.random.uniform(jax.random.fold_in(key, 11), (HEADS, SQ), jnp.float32, 1.0, 2.0)
    return (jnp.log(1.0 + position)[None, :] + margin).astype(jnp.float32)


def draw_key_codes(key, part):
    codes = jax.random.randint(jax.random.fold_in(key, 21), (SK, HEAD_DIM), -127, 128)
    return codes.astype(jnp.float32).astype(jnp.bfloat16)


def draw_value_codes(key, part):
    codes = jax.random.randint(jax.random.fold_in(key, 22), (SK, HEAD_DIM), -127, 128)
    return codes.astype(jnp.float32).astype(jnp.bfloat16)


def level_of(rng, dims, pieces, least, top_value):
    loudness, own = 1.0, jax.random.fold_in(rng, 6)
    for dim, blocks in pieces:
        steps = jnp.exp(jax.random.uniform(jax.random.fold_in(own, dim), (blocks,), jnp.float32, least / len(pieces), top_value / len(pieces)))
        loudness = loudness * jnp.repeat(steps, dims[dim] // blocks).reshape([-1 if axis == dim else 1 for axis in range(len(dims))])
    return loudness


def centred(own_key, extent, deviation, bound, shards=(), kind=jnp.bfloat16):
    loudness = level_of(own_key, extent, shards, -0.22, 0.18) if shards else 1.0
    array = jax.random.normal(own_key, extent, jnp.float32) * deviation * loudness
    return jnp.minimum(jnp.maximum(array, -bound), bound).astype(kind)


def setup_inputs(seed: int = 0) -> dict:
    key_of = jax.random.split(jax.random.key(seed), 11)
    return {
        "queries": centred(key_of[0], (SQ, HEADS * HEAD_DIM), 1.0, 6.0, ((0, 128),)),
        "d_out": centred(key_of[1], (SQ, HEADS * HEAD_DIM), 1.0, 6.0, ((0, 128),)),
        "log_sums": draw_log_sums(jax.random.fold_in(key_of[10], 71), 0),
        "deltas": centred(key_of[3], (HEADS, SQ), 0.5, 4.0, ((1, 128),), jnp.float32),
        "query_start": draw_query_start(jax.random.fold_in(key_of[10], 71), 0),
        "key_codes": draw_key_codes(jax.random.fold_in(key_of[10], 71), 0),
        "value_codes": draw_value_codes(jax.random.fold_in(key_of[10], 71), 0),
        "key_scale": jnp.clip(jnp.exp(math.log(0.02) - 2.30258502 * jax.random.uniform(key_of[7], (SK,), jnp.float32) ** level_of(key_of[7], (SK,), ((0, 128),), -0.2, 0.2)), 0.002, 0.02),
        "value_scale": jnp.clip(jnp.exp(math.log(0.02) - 2.30258502 * jax.random.uniform(key_of[8], (SK,), jnp.float32) ** level_of(key_of[8], (SK,), ((0, 128),), -0.2, 0.2)), 0.002, 0.02),
        "key_start": draw_key_start(jax.random.fold_in(key_of[10], 71), 0),
    }


def dot_nt(left, right):
    return lax.dot_general(left, right, (((1,), (1,)), ((), ())), preferred_element_type=jnp.float32)

def dot_tn(left, right):
    return lax.dot_general(left, right, (((0,), (0,)), ((), ())), preferred_element_type=jnp.float32)

def reference(queries, d_out, log_sums, deltas, query_start, key_codes, value_codes, key_scale, value_scale, key_start):
    score_scale = 1.0 / math.sqrt(HEAD_DIM)
    key_rows = (key_codes.astype(jnp.float32) * key_scale[:, None]).astype(jnp.bfloat16)
    value_rows = (value_codes.astype(jnp.float32) * value_scale[:, None]).astype(jnp.bfloat16)
    query_flat = queries.reshape(SQ * HEADS, HEAD_DIM)
    grad_flat = d_out.reshape(SQ * HEADS, HEAD_DIM)
    log_rows = log_sums.T.reshape(-1)
    delta_rows = deltas.T.reshape(-1)
    offsets = jnp.arange(BLOCK, dtype=jnp.int32)
    query_pos = (query_start[:, None] + offsets[None, :]).reshape(-1)
    row_pos = (query_pos[:, None] + jnp.zeros((1, HEADS), jnp.int32)).reshape(-1)
    key_pos = (key_start[:, None] + offsets[None, :]).reshape(-1)

    def one_tile(query_acc, tile_index):
        first = (tile_index * KTILE).astype(jnp.int32)
        tile_keys = lax.dynamic_slice_in_dim(key_rows, first, KTILE, 0)
        tile_values = lax.dynamic_slice_in_dim(value_rows, first, KTILE, 0)
        tile_pos = lax.dynamic_slice_in_dim(key_pos, first, KTILE, 0)
        scores = dot_nt(query_flat, tile_keys) * score_scale
        visible = tile_pos[None, :] <= row_pos[:, None]
        attention = jnp.where(visible, jnp.exp(scores - log_rows[:, None]), 0.0)
        attention_low = attention.astype(jnp.bfloat16)
        dprobs = dot_nt(grad_flat, tile_values)
        dscores = (attention * (dprobs - delta_rows[:, None])).astype(jnp.bfloat16)
        grad_v = dot_tn(attention_low, grad_flat)
        grad_k = dot_tn(dscores, query_flat) * score_scale
        query_acc = query_acc + jnp.dot(dscores, tile_keys, preferred_element_type=jnp.float32)
        return (query_acc, (grad_k, grad_v))
    start_acc = jnp.zeros((SQ * HEADS, HEAD_DIM), jnp.float32)
    query_acc, (tiles_k, tiles_v) = lax.scan(one_tile, start_acc, jnp.arange(N_KA, dtype=jnp.int32))
    grad_queries = (query_acc * score_scale).reshape(SQ, HEADS * HEAD_DIM).astype(jnp.bfloat16)
    grad_keys = tiles_k.reshape(SK, HEAD_DIM).astype(jnp.bfloat16)
    grad_values = tiles_v.reshape(SK, HEAD_DIM).astype(jnp.bfloat16)
    return (grad_queries, grad_keys, grad_values)
```

```python
import math

import jax
import jax.numpy as jnp
from jax import lax
from jax.experimental import pallas as pl
from jax.experimental.pallas import tpu as pltpu
from jax.sharding import PartitionSpec as P

HEADS = 8
HEAD_DIM = 128
MESSAGES = 67
SCALE = 1.0 / math.sqrt(HEAD_DIM)
LOG2E = math.log2(math.e)
MESH = pl.DeviceIdType.MESH
BF16 = jnp.bfloat16
F32 = jnp.float32

STEPS = [(c, t) for c in (0, 1, 3, 2) for t in (0, 1, 3, 2)]


def dot(a, b, ca, cb):
    return lax.dot_general(a, b, (((ca,), (cb,)), ((), ())), preferred_element_type=F32)


def pick(table, s):
    value = jnp.int32(table[0])
    for i, entry in enumerate(table[1:], 1):
        value = jnp.where(s == i, jnp.int32(entry), value)
    return value


def flip(bit, by):
    return bit + by - 2 * bit * by


def kernel(
    q_hbm,
    o_hbm,
    log_ref,
    delta_ref,
    qstart_ref,
    kcode_ref,
    vcode_ref,
    kscale_ref,
    vscale_ref,
    kstart_ref,
    gq_ref,
    gk_ref,
    gv_ref,
    qo,
    ld,
    kv,
    dq_acc,
    dk_acc,
    dv_acc,
    p_t,
    ds_t,
    diff,
    dq_sib,
    dq_sib_in,
    dq_two,
    dq_two_in,
    dq_one,
    dq_one_in,
    dq_z,
    dq_z_in,
    kv_two,
    kv_two_in,
    kv_one,
    kv_one_in,
    kv_z,
    kv_z_in,
    send_sems,
    recv_sems,
    local_sems,
):
    g = lax.axis_index("pb")
    k = lax.axis_index("ka")
    zh, y = g // 4, g % 4
    zl, x, core = k // 8, (k // 2) % 4, k % 2

    def at_ka(dx, dz, dc):
        return flip(zl, dz) * 8 + ((x + dx) % 4) * 2 + flip(core, dc)

    def at_pb(dy, dz):
        return flip(zh, dz) * 4 + (y + dy) % 4

    near = {
        "sib": (g, at_ka(0, 0, 1)),
        "x+": (g, at_ka(1, 0, 0)),
        "x-": (g, at_ka(3, 0, 0)),
        "zl": (g, at_ka(0, 1, 0)),
        "y+": (at_pb(1, 0), k),
        "y-": (at_pb(3, 0), k),
        "zh": (at_pb(0, 1), k),
    }
    barrier = pltpu.get_barrier_semaphore()
    for to in near.values():
        pl.semaphore_signal(barrier, inc=1, device_id=to, device_id_type=MESH)

    messages = {}

    def message(name, src, dst, to):
        i = len(messages)
        assert name not in messages
        messages[name] = lambda: pltpu.make_async_remote_copy(
            src_ref=src,
            dst_ref=dst,
            send_sem=send_sems.at[i],
            recv_sem=recv_sems.at[i],
            device_id=near[to],
            device_id_type=MESH,
        )

    def send(*names):
        for name in names:
            messages[name]().start()

    def arrived(*names):
        for name in names:
            messages[name]().wait_recv()

    def slot(dx, dz, dc=0):
        return dx * 4 + dz * 2 + dc

    for dz in (0, 1):
        own = slot(0, dz)
        for to, dx in (("x+", 3), ("x-", 1)):
            message(f"q{dz}{to}", qo.at[own], qo.at[slot(dx, dz)], to)
            message(f"l{dz}{to}", ld.at[own], ld.at[slot(dx, dz)], to)
        message(f"q{dz}2+", qo.at[slot(3, dz), 0], qo.at[slot(2, dz), 0], "x+")
        message(f"q{dz}2-", qo.at[slot(1, dz), 1], qo.at[slot(2, dz), 1], "x-")
        message(f"l{dz}2-", ld.at[slot(1, dz)], ld.at[slot(2, dz)], "x-")
        for dx in range(4):
            message(f"q{dz}s{dx}", qo.at[slot(dx, dz)], qo.at[slot(dx, dz, 1)], "sib")
            message(f"l{dz}s{dx}", ld.at[slot(dx, dz)], ld.at[slot(dx, dz, 1)], "sib")
    message("qz", qo.at[slot(0, 0)], qo.at[slot(0, 1)], "zl")
    message("lz", ld.at[slot(0, 0)], ld.at[slot(0, 1)], "zl")
    for dz in (0, 1):
        message(f"k{dz}y+", kv.at[dz], kv.at[6 + dz], "y+")
        message(f"k{dz}y-", kv.at[dz], kv.at[2 + dz], "y-")
        message(f"k{dz}2+", kv.at[6 + dz, 0], kv.at[4 + dz, 0], "y+")
        message(f"k{dz}2-", kv.at[2 + dz, 1], kv.at[4 + dz, 1], "y-")
    message("kz", kv.at[0], kv.at[1], "zh")
    for dz in (0, 1):
        for dx in range(4):
            message(f"dq{dz}s{dx}", dq_sib.at[dx, dz], dq_sib_in.at[dx, dz], "sib")
        message(f"dq{dz}2+", dq_two.at[dz, pl.ds(0, 64)], dq_two_in.at[dz, pl.ds(0, 64)], "x+")
        message(f"dq{dz}2-", dq_two.at[dz, pl.ds(64, 64)], dq_two_in.at[dz, pl.ds(64, 64)], "x-")
        message(f"dq{dz}1+", dq_one.at[0, dz], dq_one_in.at[0, dz], "x+")
        message(f"dq{dz}1-", dq_one.at[1, dz], dq_one_in.at[1, dz], "x-")
    message("dqz", dq_z, dq_z_in, "zl")
    for dz in (0, 1):
        message(f"dk{dz}2+", kv_two.at[0, dz], kv_two_in.at[0, dz], "y+")
        message(f"dk{dz}2-", kv_two.at[1, dz], kv_two_in.at[1, dz], "y-")
        message(f"dk{dz}1+", kv_one.at[0, dz], kv_one_in.at[0, dz], "y+")
        message(f"dk{dz}1-", kv_one.at[1, dz], kv_one_in.at[1, dz], "y-")
    message("dkz", kv_z, kv_z_in, "zh")
    assert len(messages) == MESSAGES, len(messages)

    local = [
        pltpu.make_async_copy(q_hbm, qo.at[0, 0], local_sems.at[0]),
        pltpu.make_async_copy(o_hbm, qo.at[0, 1], local_sems.at[1]),
    ]
    for copy in local:
        copy.start()
    ld[0, 0:1, :] = jnp.concatenate([log_ref[h : h + 1, :] for h in range(HEADS)], axis=1) * LOG2E
    ld[0, 1:2, :] = jnp.concatenate([delta_ref[h : h + 1, :] for h in range(HEADS)], axis=1)
    ld[0, 2:8, :] = jnp.zeros((6, 256), F32)
    for i, (codes, factors) in enumerate(((kcode_ref, kscale_ref), (vcode_ref, vscale_ref))):
        for half in (0, 1):
            rows = pl.ds(half * 128, 128)
            factor = jnp.broadcast_to(factors[half : half + 1, :], (128, 128)).T
            kv[0, i, rows, :] = (codes[rows, :].astype(F32) * factor).astype(BF16)
    diff[...] = lax.broadcasted_iota(jnp.int32, (128, 256), 0) - lax.broadcasted_iota(jnp.int32, (128, 256), 1) % 32
    dq_acc[...] = jnp.zeros_like(dq_acc)
    dk_acc[...] = jnp.zeros_like(dk_acc)
    dv_acc[...] = jnp.zeros_like(dv_acc)
    for copy in local:
        copy.wait()
    pl.semaphore_wait(barrier, len(near))

    def spread_own():
        send("kz", "k0y+", "k0y-", "qz", "lz", "q0x+", "l0x+", "q0x-", "l0x-", "q0s0", "l0s0")

    def have_q(dz):
        if dz:
            arrived("qz", "lz")
            send("q1x+", "l1x+", "q1x-", "l1x-", "q1s0", "l1s0")

    def have_k(dz):
        if dz:
            arrived("kz")
            send("k1y+", "k1y-")

    def relay_q(dz):
        arrived(f"q{dz}x+", f"l{dz}x+")
        send(f"q{dz}2+", f"q{dz}s3", f"l{dz}s3")
        arrived(f"q{dz}x-", f"l{dz}x-")
        send(f"q{dz}2-", f"l{dz}2-", f"q{dz}s1", f"l{dz}s1")

    def relay_k(dz):
        arrived(f"k{dz}y+")
        send(f"k{dz}2+")
        arrived(f"k{dz}y-")
        send(f"k{dz}2-")

    def last_q(dz):
        arrived(f"q{dz}2+", f"q{dz}2-", f"l{dz}2-")
        send(f"q{dz}s2", f"l{dz}s2")

    def last_k(dz):
        arrived(f"k{dz}2+", f"k{dz}2-")

    def twin_q(dx):
        arrived(f"q0s{dx}", f"l0s{dx}", f"q1s{dx}", f"l1s{dx}")

    def dq_part(dx, dz, dc):
        at = (dz * 2 + dc) * 256
        return dq_acc[dx, :, at : at + 256]

    def dq_swap(dx):
        for dz in (0, 1):
            dq_sib[dx, dz] = dq_part(dx, dz, 1).astype(BF16)
        send(f"dq0s{dx}", f"dq1s{dx}")

    def dq_both(dx, dz):
        arrived(f"dq{dz}s{dx}")
        return dq_part(dx, dz, 0) + dq_sib_in[dx, dz].astype(F32)

    def dq_far():
        for dz in (0, 1):
            dq_two[dz] = dq_both(2, dz).astype(BF16)
        for dz in (0, 1):
            send(f"dq{dz}2+", f"dq{dz}2-")

    def dq_next(way):
        dx, sign, top = ((1, "+", 0), (3, "-", 64))[way]
        for dz in (0, 1):
            total = dq_both(dx, dz)
            arrived(f"dq{dz}2{sign}")
            more = dq_two_in[dz, top : top + 64].astype(F32)
            dq_one[way, dz, top : top + 64] = (total[top : top + 64] + more).astype(BF16)
            dq_one[way, dz, 64 - top : 128 - top] = total[64 - top : 128 - top].astype(BF16)
        send(f"dq01{sign}", f"dq11{sign}")

    def dq_here(dz):
        total = dq_both(0, dz)
        arrived(f"dq{dz}1+", f"dq{dz}1-")
        return total + dq_one_in[0, dz].astype(F32) + dq_one_in[1, dz].astype(F32)

    def dq_cross():
        dq_z[...] = dq_here(1).astype(BF16)
        send("dqz")

    def dq_final():
        total = dq_here(0)
        arrived("dqz")
        total = ((total + dq_z_in[...].astype(F32)) * SCALE).T
        for h in range(HEADS):
            gq_ref[:, h * 128 : (h + 1) * 128] = total[h * 32 : (h + 1) * 32].astype(BF16)

    def dk_part(acc, dy, dz):
        return acc[dy, dz * 256 : (dz + 1) * 256]

    def dk_far():
        for dz in (0, 1):
            kv_two[0, dz] = dk_part(dk_acc, 2, dz).astype(BF16)
            kv_two[1, dz] = dk_part(dv_acc, 2, dz).astype(BF16)
        for dz in (0, 1):
            send(f"dk{dz}2+", f"dk{dz}2-")

    def dk_next(way):
        dy, sign = ((1, "+"), (3, "-"))[way]
        accs = (dk_acc, dv_acc)
        for dz in (0, 1):
            arrived(f"dk{dz}2{sign}")
            kv_one[way, dz, way] = (dk_part(accs[way], dy, dz) + kv_two_in[way, dz].astype(F32)).astype(BF16)
            kv_one[way, dz, 1 - way] = dk_part(accs[1 - way], dy, dz).astype(BF16)
        for dz in (0, 1):
            send(f"dk{dz}1{sign}")

    def dk_here(dz):
        arrived(f"dk{dz}1+", f"dk{dz}1-")
        return [
            dk_part(acc, 0, dz) + kv_one_in[0, dz, i].astype(F32) + kv_one_in[1, dz, i].astype(F32)
            for i, acc in enumerate((dk_acc, dv_acc))
        ]

    def dk_cross():
        for i, total in enumerate(dk_here(1)):
            kv_z[i] = total.astype(BF16)
        send("dkz")

    def dk_final():
        keys, values = dk_here(0)
        arrived("dkz")
        gk_ref[...] = ((keys + kv_z_in[0].astype(F32)) * SCALE).astype(BF16)
        gv_ref[...] = (values + kv_z_in[1].astype(F32)).astype(BF16)

    spread_own()
    have_q(1)
    relay_q(0)
    relay_k(0)
    have_k(1)
    last_q(0)
    last_k(0)
    relay_q(1)
    relay_k(1)
    last_q(1)
    last_k(1)
    for dx in range(4):
        twin_q(dx)

    def one_step(s, carry):
        c, t = pick([step[0] for step in STEPS], s), pick([step[1] for step in STEPS], s)
        keys = jnp.concatenate([kv[2 * c, 0], kv[2 * c + 1, 0]], axis=0)
        values = jnp.concatenate([kv[2 * c, 1], kv[2 * c + 1, 1]], axis=0)
        starts = []
        for dz in (0, 1):
            owner = flip(zh, dz) * 4 + (y + c) % 4
            starts += [kstart_ref[owner * 2], kstart_ref[owner * 2 + 1]]
        offset = diff[...]
        all_q, all_o = [], []
        for j in range(4):
            piece = t * 4 + j
            owner = flip(zl, j // 2) * 8 + ((x + t) % 4) * 2 + flip(core, j % 2)
            first = qstart_ref[owner // 4] + (owner % 4) * 32
            q_rows = jnp.concatenate([qo[piece, 0, :, h * 128 : (h + 1) * 128] for h in range(HEADS)], axis=0)
            o_rows = jnp.concatenate([qo[piece, 1, :, h * 128 : (h + 1) * 128] for h in range(HEADS)], axis=0)
            logs, deltas = ld[piece, 0:1, :], ld[piece, 1:2, :]
            scores = dot(keys, q_rows, 1, 1)
            dprobs = dot(values, o_rows, 1, 1)
            visible = jnp.concatenate([offset <= first - start for start in starts], axis=0)
            attention = jnp.where(visible, jnp.exp2(scores * (SCALE * LOG2E) - logs), 0.0)
            columns = pl.ds(j * 256, 256)
            p_t[:, columns] = attention.astype(BF16)
            ds_t[:, columns] = (attention * (dprobs - deltas)).astype(BF16)
            all_q.append(q_rows)
            all_o.append(o_rows)
        dv_acc[c] += dot(p_t[...], jnp.concatenate(all_o, axis=0), 1, 0)
        dk_acc[c] += dot(ds_t[...], jnp.concatenate(all_q, axis=0), 1, 0)
        dq_acc[t] += dot(keys.T, ds_t[...], 1, 0)
        return carry

    lax.fori_loop(0, len(STEPS), one_step, 0)

    for dx in (2, 1, 3, 0):
        dq_swap(dx)
    dk_far()
    dq_far()
    dk_next(0)
    dk_next(1)
    dq_next(0)
    dq_next(1)
    dk_cross()
    dq_cross()
    dk_final()
    dq_final()
    for make in messages.values():
        make().wait_send()


def local(
    queries, d_out, log_sums, deltas, query_start, key_codes, value_codes, key_scale, value_scale, key_start
):
    vmem = pl.BlockSpec(memory_space=pltpu.VMEM)
    smem = pl.BlockSpec(memory_space=pltpu.SMEM)
    anywhere = pl.BlockSpec(memory_space=pl.ANY)
    piece = (128, 256)
    return pl.pallas_call(
        kernel,
        out_shape=(
            jax.ShapeDtypeStruct((32, 1024), BF16),
            jax.ShapeDtypeStruct((256, 128), BF16),
            jax.ShapeDtypeStruct((256, 128), BF16),
        ),
        in_specs=[anywhere, anywhere, vmem, vmem, smem, vmem, vmem, vmem, vmem, smem],
        out_specs=[vmem, vmem, vmem],
        scratch_shapes=[
            pltpu.VMEM((16, 2, 32, 1024), BF16),
            pltpu.VMEM((16, 8, 256), F32),
            pltpu.VMEM((8, 2, 256, 128), BF16),
            pltpu.VMEM((4, 128, 1024), F32),
            pltpu.VMEM((4, 512, 128), F32),
            pltpu.VMEM((4, 512, 128), F32),
            pltpu.VMEM((512, 1024), BF16),
            pltpu.VMEM((512, 1024), BF16),
            pltpu.VMEM((128, 256), jnp.int32),
            pltpu.VMEM((4, 2, *piece), BF16),
            pltpu.VMEM((4, 2, *piece), BF16),
            pltpu.VMEM((2, *piece), BF16),
            pltpu.VMEM((2, *piece), BF16),
            pltpu.VMEM((2, 2, *piece), BF16),
            pltpu.VMEM((2, 2, *piece), BF16),
            pltpu.VMEM(piece, BF16),
            pltpu.VMEM(piece, BF16),
            pltpu.VMEM((2, 2, 256, 128), BF16),
            pltpu.VMEM((2, 2, 256, 128), BF16),
            pltpu.VMEM((2, 2, 2, 256, 128), BF16),
            pltpu.VMEM((2, 2, 2, 256, 128), BF16),
            pltpu.VMEM((2, 256, 128), BF16),
            pltpu.VMEM((2, 256, 128), BF16),
            pltpu.SemaphoreType.DMA((MESSAGES,)),
            pltpu.SemaphoreType.DMA((MESSAGES,)),
            pltpu.SemaphoreType.DMA((2,)),
        ],
        compiler_params=pltpu.CompilerParams(
            collective_id=0, has_side_effects=True, vmem_limit_bytes=60 << 20
        ),
        name="fused",
    )(
        queries,
        d_out,
        log_sums,
        deltas,
        query_start,
        key_codes,
        value_codes,
        key_scale.reshape(2, 128),
        value_scale.reshape(2, 128),
        key_start,
    )


def solution(mesh):
    placed = (
        P(("pb", "ka"), None),
        P(("pb", "ka"), None),
        P(None, ("pb", "ka")),
        P(None, ("pb", "ka")),
        P("pb"),
        P(("ka", "pb"), None),
        P(("ka", "pb"), None),
        P(("ka", "pb")),
        P(("ka", "pb")),
        P("ka"),
    )
    return jax.shard_map(
        local,
        mesh=mesh,
        in_specs=placed,
        out_specs=(P(("pb", "ka"), None), P(("ka", "pb"), None), P(("ka", "pb"), None)),
        check_vma=False,
    )
```

```python
import math

import jax
import jax.numpy as jnp
from jax import lax
from jax.experimental import pallas as pl
from jax.experimental.pallas import tpu as pltpu
from jax.sharding import PartitionSpec as P

HEADS = 8
HEAD_DIM = 128
SCALE = 1.0 / math.sqrt(HEAD_DIM)
LOG2E = math.log2(math.e)
MESH = pl.DeviceIdType.MESH
BF16 = jnp.bfloat16
F32 = jnp.float32

TILES = (((0, 0), (1, 0), (3, 0), (0, 1)), ((2, 0), (1, 1), (3, 1), (2, 1)))
CHUNKS = (((0, 0), (0, 1)), ((1, 0), (3, 0)), ((1, 1), (3, 1)), ((2, 0), (2, 1)))
STEPS = (
    (0, 0), (1, 0), (0, 1), (1, 1), (2, 0), (2, 1), (3, 0), (3, 1),
    (3, 2), (3, 3), (2, 3), (2, 2), (1, 3), (0, 3), (1, 2), (0, 2),
)
HAND_OVER = {(0, 1): 0, (1, 0): 0, (3, 0): 0, (2, 0): 4, (1, 1): 5, (3, 1): 5, (2, 1): 7}
OFFSETS = tuple((d, dz) for dz in (0, 1) for d in (0, 1, 3, 2))
AWAY = OFFSETS[1:]
N_MESSAGES = 60


def place(groups, piece):
    for i, group in enumerate(groups):
        if piece in group:
            return i, group.index(piece)


def last_step(column, index):
    return max(i for i, step in enumerate(STEPS) if step[column] == index)


def dot(a, b, ca, cb):
    return lax.dot_general(a, b, (((ca,), (cb,)), ((), ())), preferred_element_type=F32)


def pick(table, s):
    value = jnp.int32(table[0])
    for i, entry in enumerate(table[1:], 1):
        value = jnp.where(s == i, jnp.int32(entry), value)
    return value


def flip(bit, by):
    return bit + by - 2 * bit * by


def kernel(
    q_hbm,
    o_hbm,
    log_ref,
    delta_ref,
    qstart_ref,
    kcode_ref,
    vcode_ref,
    kscale_ref,
    vscale_ref,
    kstart_ref,
    gq_ref,
    gk_ref,
    gv_ref,
    qo,
    ld,
    kv,
    dq_acc,
    dk_acc,
    dv_acc,
    p_t,
    ds_t,
    diff,
    dq_swap,
    dq_swapped,
    dq_out,
    dq_in,
    dkv_out,
    dkv_in,
    send_sems,
    recv_sems,
    local_sems,
):
    g = lax.axis_index("pb")
    k = lax.axis_index("ka")
    zh, y = g // 4, g % 4
    zl, x, core = k // 8, (k // 2) % 4, k % 2

    def query_owner(dx, dz, dc=0):
        return flip(zl, dz) * 8 + ((x + dx) % 4) * 2 + flip(core, dc)

    def key_owner(dy, dz):
        return flip(zh, dz) * 4 + (y + dy) % 4

    sibling = (g, query_owner(0, 0, 1))
    query_peer = {piece: (g, query_owner(*piece)) for piece in AWAY}
    key_peer = {piece: (key_owner(*piece), k) for piece in AWAY}
    peers = [sibling, *query_peer.values(), *key_peer.values()]
    barrier = pltpu.get_barrier_semaphore()
    for to in peers:
        pl.semaphore_signal(barrier, inc=1, device_id=to, device_id_type=MESH)

    messages, sent = {}, []

    def message(name, src, dst, to):
        i = len(messages)
        assert name not in messages and i < N_MESSAGES
        messages[name] = lambda: pltpu.make_async_remote_copy(
            src_ref=src,
            dst_ref=dst,
            send_sem=send_sems.at[i],
            recv_sem=recv_sems.at[i],
            device_id=to,
            device_id_type=MESH,
        )

    def send(*names):
        for name in names:
            sent.append(name)
            messages[name]().start()

    def arrived(*names):
        for name in names:
            messages[name]().wait_recv()

    def query_slot(piece, dc=0):
        half, at = place(TILES, piece)
        return (half * 2 + dc) * 4 + at

    def key_slot(piece):
        chunk, at = place(CHUNKS, piece)
        return chunk * 2 + at

    def back(piece):
        return (-piece[0]) % 4, piece[1]

    here = (0, 0)
    for dx in (1, 3, 2):
        for dz in (0, 1):
            to = query_peer[dx, 0]
            message(f"q{dx}{dz}", qo.at[query_slot((0, dz))], qo.at[query_slot(back((dx, dz)))], to)
            message(f"l{dx}{dz}", ld.at[query_slot((0, dz))], ld.at[query_slot(back((dx, dz)))], to)
            message(f"k{dx}{dz}", kv.at[key_slot((0, dz))], kv.at[key_slot(back((dx, dz)))], key_peer[dx, 0])
    message("q01", qo.at[query_slot(here)], qo.at[query_slot((0, 1))], query_peer[0, 1])
    message("l01", ld.at[query_slot(here)], ld.at[query_slot((0, 1))], query_peer[0, 1])
    message("k01", kv.at[key_slot(here)], kv.at[key_slot((0, 1))], key_peer[0, 1])
    for piece in OFFSETS:
        dx, dz = piece
        message(f"hq{dx}{dz}", qo.at[query_slot(piece)], qo.at[query_slot(piece, 1)], sibling)
        message(f"hl{dx}{dz}", ld.at[query_slot(piece)], ld.at[query_slot(piece, 1)], sibling)
    for half in (0, 1):
        message(f"sq{half}", dq_swap.at[half], dq_swapped.at[half], sibling)
    for i, piece in enumerate(AWAY):
        message(f"dq{piece[0]}{piece[1]}", dq_out.at[i], dq_in.at[i], query_peer[piece])
        message(f"dk{piece[0]}{piece[1]}", dkv_out.at[i], dkv_in.at[i], key_peer[piece])

    local = [
        pltpu.make_async_copy(q_hbm, qo.at[0, 0], local_sems.at[0]),
        pltpu.make_async_copy(o_hbm, qo.at[0, 1], local_sems.at[1]),
    ]
    for copy in local:
        copy.start()
    ld[0, 0:1, :] = jnp.concatenate([log_ref[h : h + 1, :] for h in range(HEADS)], axis=1) * LOG2E
    ld[0, 1:2, :] = jnp.concatenate([delta_ref[h : h + 1, :] for h in range(HEADS)], axis=1)
    ld[0, 2:8, :] = jnp.zeros((6, 256), F32)
    for i, (codes, factors) in enumerate(((kcode_ref, kscale_ref), (vcode_ref, vscale_ref))):
        for half in (0, 1):
            rows = pl.ds(half * 128, 128)
            factor = jnp.broadcast_to(factors[half : half + 1, :], (128, 128)).T
            kv[0, i, rows, :] = (codes[rows, :].astype(F32) * factor).astype(BF16)
    diff[...] = lax.broadcasted_iota(jnp.int32, (128, 256), 0) - lax.broadcasted_iota(jnp.int32, (128, 256), 1) % 32
    dq_acc[...] = jnp.zeros_like(dq_acc)
    dk_acc[...] = jnp.zeros_like(dk_acc)
    dv_acc[...] = jnp.zeros_like(dv_acc)
    for copy in local:
        copy.wait()
    pl.semaphore_wait(barrier, len(peers))

    send("k01", "q01", "l01", "k10", "k30", "q10", "l10", "q30", "l30", "hq00", "hl00", "k20", "q20", "l20")
    arrived("q01", "l01")
    send("q11", "l11", "q31", "l31", "q21", "l21")
    arrived("k01")
    send("k11", "k31", "k21")

    def came(letters, piece):
        dx, dz = back(piece)
        arrived(*(f"{letter}{dx}{dz}" for letter in letters))

    have = {"q01", "k01"}

    def need(letters, piece):
        name = f"{letters[0]}{piece[0]}{piece[1]}"
        if piece != here and name not in have:
            have.add(name)
            came(letters, piece)

    def hand_over(piece):
        need("ql", piece)
        send(f"hq{piece[0]}{piece[1]}", f"hl{piece[0]}{piece[1]}")

    def ready(step):
        for piece, at in HAND_OVER.items():
            if at == step:
                hand_over(piece)
        chunk, tile = STEPS[step]
        if all(before[0] != chunk for before in STEPS[:step]):
            for piece in CHUNKS[chunk]:
                need("k", piece)
        if all(before[1] != tile for before in STEPS[:step]):
            for piece in TILES[tile // 2]:
                if tile % 2:
                    arrived(f"hq{piece[0]}{piece[1]}", f"hl{piece[0]}{piece[1]}")
                else:
                    need("ql", piece)

    def query_part(piece, dc=0):
        half, at = place(TILES, piece)
        return dq_acc[half * 2 + dc, :, at * 256 : (at + 1) * 256]

    def query_sum(piece):
        half, at = place(TILES, piece)
        return query_part(piece) + dq_swapped[half, at].astype(F32)

    def key_part(acc, piece):
        chunk, at = place(CHUNKS, piece)
        return acc[chunk, at * 256 : (at + 1) * 256]

    def done(step):
        for chunk in range(4):
            if last_step(0, chunk) == step:
                pieces = [piece for piece in CHUNKS[chunk] if piece != here]
                for piece in pieces:
                    for n, acc in enumerate((dk_acc, dv_acc)):
                        dkv_out[AWAY.index(piece), n] = key_part(acc, piece).astype(BF16)
                send(*(f"dk{piece[0]}{piece[1]}" for piece in reversed(pieces)))
        for half in (0, 1):
            first, second = last_step(1, half * 2), last_step(1, half * 2 + 1)
            if second == step:
                for at, piece in enumerate(TILES[half]):
                    dq_swap[half, at] = query_part(piece, 1).astype(BF16)
                send(f"sq{half}")
            if max(first, second + 1) == step or max(first, second + 1) == len(STEPS) == step + 1:
                arrived(f"sq{half}")
                pieces = [piece for piece in TILES[half] if piece != here]
                for piece in reversed(pieces):
                    dq_out[AWAY.index(piece)] = query_sum(piece).astype(BF16)
                send(*(f"dq{piece[0]}{piece[1]}" for piece in reversed(pieces)))

    def one_step(s, carry):
        for step in range(len(STEPS)):
            pl.when(s == step)(lambda step=step: ready(step))
        c, t = pick([step[0] for step in STEPS], s), pick([step[1] for step in STEPS], s)
        keys = jnp.concatenate([kv[2 * c, 0], kv[2 * c + 1, 0]], axis=0)
        values = jnp.concatenate([kv[2 * c, 1], kv[2 * c + 1, 1]], axis=0)
        starts = []
        for at in (0, 1):
            owner = key_owner(pick([chunk[at][0] for chunk in CHUNKS], c), pick([chunk[at][1] for chunk in CHUNKS], c))
            starts += [kstart_ref[owner * 2], kstart_ref[owner * 2 + 1]]
        offset = diff[...]
        all_q, all_o = [], []
        for at in range(4):
            piece = t * 4 + at
            half = t // 2
            owner = query_owner(
                pick([tile[at][0] for tile in TILES], half), pick([tile[at][1] for tile in TILES], half), t % 2
            )
            first = qstart_ref[owner // 4] + (owner % 4) * 32
            q_rows = jnp.concatenate([qo[piece, 0, :, h * 128 : (h + 1) * 128] for h in range(HEADS)], axis=0)
            o_rows = jnp.concatenate([qo[piece, 1, :, h * 128 : (h + 1) * 128] for h in range(HEADS)], axis=0)
            logs, deltas = ld[piece, 0:1, :], ld[piece, 1:2, :]
            scores = dot(keys, q_rows, 1, 1)
            dprobs = dot(values, o_rows, 1, 1)
            visible = jnp.concatenate([offset <= first - start for start in starts], axis=0)
            attention = jnp.where(visible, jnp.exp2(scores * (SCALE * LOG2E) - logs), 0.0)
            columns = pl.ds(at * 256, 256)
            p_t[:, columns] = attention.astype(BF16)
            ds_t[:, columns] = (attention * (dprobs - deltas)).astype(BF16)
            all_q.append(q_rows)
            all_o.append(o_rows)
        dv_acc[c] += dot(p_t[...], jnp.concatenate(all_o, axis=0), 1, 0)
        dk_acc[c] += dot(ds_t[...], jnp.concatenate(all_q, axis=0), 1, 0)
        dq_acc[t] += dot(keys.T, ds_t[...], 1, 0)
        for step in range(len(STEPS)):
            pl.when(s == step)(lambda step=step: done(step))
        return carry

    lax.fori_loop(0, len(STEPS), one_step, 0)

    keys, values = key_part(dk_acc, here), key_part(dv_acc, here)
    for i, piece in enumerate(AWAY):
        arrived(f"dk{piece[0]}{piece[1]}")
        keys += dkv_in[i, 0].astype(F32)
        values += dkv_in[i, 1].astype(F32)
    gk_ref[...] = (keys * SCALE).astype(BF16)
    gv_ref[...] = values.astype(BF16)
    total = query_sum(here)
    for i, piece in enumerate(AWAY):
        arrived(f"dq{piece[0]}{piece[1]}")
        total += dq_in[i].astype(F32)
    total = (total * SCALE).T
    for h in range(HEADS):
        gq_ref[:, h * 128 : (h + 1) * 128] = total[h * 32 : (h + 1) * 32].astype(BF16)
    assert sorted(sent) == sorted(messages), set(messages) ^ set(sent)
    for make in messages.values():
        make().wait_send()


def local(
    queries, d_out, log_sums, deltas, query_start, key_codes, value_codes, key_scale, value_scale, key_start
):
    vmem = pl.BlockSpec(memory_space=pltpu.VMEM)
    smem = pl.BlockSpec(memory_space=pltpu.SMEM)
    anywhere = pl.BlockSpec(memory_space=pl.ANY)
    piece = (128, 256)
    return pl.pallas_call(
        kernel,
        out_shape=(
            jax.ShapeDtypeStruct((32, 1024), BF16),
            jax.ShapeDtypeStruct((256, 128), BF16),
            jax.ShapeDtypeStruct((256, 128), BF16),
        ),
        in_specs=[anywhere, anywhere, vmem, vmem, smem, vmem, vmem, vmem, vmem, smem],
        out_specs=[vmem, vmem, vmem],
        scratch_shapes=[
            pltpu.VMEM((16, 2, 32, 1024), BF16),
            pltpu.VMEM((16, 8, 256), F32),
            pltpu.VMEM((8, 2, 256, 128), BF16),
            pltpu.VMEM((4, 128, 1024), F32),
            pltpu.VMEM((4, 512, 128), F32),
            pltpu.VMEM((4, 512, 128), F32),
            pltpu.VMEM((512, 1024), BF16),
            pltpu.VMEM((512, 1024), BF16),
            pltpu.VMEM((128, 256), jnp.int32),
            pltpu.VMEM((2, 4, *piece), BF16),
            pltpu.VMEM((2, 4, *piece), BF16),
            pltpu.VMEM((7, *piece), BF16),
            pltpu.VMEM((7, *piece), BF16),
            pltpu.VMEM((7, 2, 256, 128), BF16),
            pltpu.VMEM((7, 2, 256, 128), BF16),
            pltpu.SemaphoreType.DMA((N_MESSAGES,)),
            pltpu.SemaphoreType.DMA((N_MESSAGES,)),
            pltpu.SemaphoreType.DMA((2,)),
        ],
        compiler_params=pltpu.CompilerParams(
            collective_id=0, has_side_effects=True, vmem_limit_bytes=60 << 20
        ),
        name="fused",
    )(
        queries,
        d_out,
        log_sums,
        deltas,
        query_start,
        key_codes,
        value_codes,
        key_scale.reshape(2, 128),
        value_scale.reshape(2, 128),
        key_start,
    )


def solution(mesh):
    placed = (
        P(("pb", "ka"), None),
        P(("pb", "ka"), None),
        P(None, ("pb", "ka")),
        P(None, ("pb", "ka")),
        P("pb"),
        P(("ka", "pb"), None),
        P(("ka", "pb"), None),
        P(("ka", "pb")),
        P(("ka", "pb")),
        P("ka"),
    )
    return jax.shard_map(
        local,
        mesh=mesh,
        in_specs=placed,
        out_specs=(P(("pb", "ka"), None), P(("ka", "pb"), None), P(("ka", "pb"), None)),
        check_vma=False,
    )
```

```python
import math

import jax
import jax.numpy as jnp
from jax import lax
from jax.experimental import pallas as pl
from jax.experimental.pallas import tpu as pltpu
from jax.sharding import PartitionSpec as P

HEADS = 8
HEAD_DIM = 128
SCALE = 1.0 / math.sqrt(HEAD_DIM)
LOG2E = math.log2(math.e)
MESH = pl.DeviceIdType.MESH
BF16 = jnp.bfloat16
F32 = jnp.float32

TILES = (((0, 0), (1, 0), (3, 0), (0, 1)), ((2, 0), (1, 1), (3, 1), (2, 1)))
CHUNKS = (((0, 0), (0, 1)), ((1, 0), (3, 0)), ((1, 1), (3, 1)), ((2, 0), (2, 1)))
STEPS = (
    (1, 0), (0, 0), (1, 1), (0, 1), (2, 0), (2, 1), (2, 2), (3, 0),
    (2, 3), (3, 1), (3, 3), (3, 2), (0, 3), (0, 2), (1, 3), (1, 2),
)
CROSS = 14
HAND_OVER = { (2, 0): 4, (1, 1): 5, (3, 1): 5, (2, 1): 6}
OFFSETS = tuple((d, dz) for dz in (0, 1) for d in (0, 1, 3, 2))
AWAY = OFFSETS[1:]
N_MESSAGES = 60


def place(groups, piece):
    for i, group in enumerate(groups):
        if piece in group:
            return i, group.index(piece)


def last_step(column, index):
    return max(i for i, step in enumerate(STEPS) if step[column] == index)


def dot(a, b, ca, cb):
    return lax.dot_general(a, b, (((ca,), (cb,)), ((), ())), preferred_element_type=F32)


def pick(table, s):
    value = jnp.int32(table[0])
    for i, entry in enumerate(table[1:], 1):
        value = jnp.where(s == i, jnp.int32(entry), value)
    return value


def flip(bit, by):
    return bit + by - 2 * bit * by


def kernel(
    q_hbm,
    o_hbm,
    log_ref,
    delta_ref,
    qstart_ref,
    kcode_ref,
    vcode_ref,
    kscale_ref,
    vscale_ref,
    kstart_ref,
    gq_ref,
    gk_ref,
    gv_ref,
    qo,
    ld,
    kv,
    dq_acc,
    dk_acc,
    dv_acc,
    p_t,
    ds_t,
    diff,
    dq_swap,
    dq_swapped,
    dq_out,
    dq_in,
    dkv_out,
    dkv_in,
    send_sems,
    recv_sems,
    local_sems,
):
    g = lax.axis_index("pb")
    k = lax.axis_index("ka")
    zh, y = g // 4, g % 4
    zl, x, core = k // 8, (k // 2) % 4, k % 2

    def query_owner(dx, dz, dc=0):
        return flip(zl, dz) * 8 + ((x + dx) % 4) * 2 + flip(core, dc)

    def key_owner(dy, dz):
        return flip(zh, dz) * 4 + (y + dy) % 4

    sibling = (g, query_owner(0, 0, 1))
    query_peer = {piece: (g, query_owner(*piece)) for piece in AWAY}
    key_peer = {piece: (key_owner(*piece), k) for piece in AWAY if 0 in piece}
    peers = [sibling, *query_peer.values(), *key_peer.values()]
    barrier = pltpu.get_barrier_semaphore()
    for to in peers:
        pl.semaphore_signal(barrier, inc=1, device_id=to, device_id_type=MESH)

    messages, sent = {}, []

    def message(name, src, dst, to):
        i = len(messages)
        assert name not in messages and i < N_MESSAGES
        messages[name] = lambda: pltpu.make_async_remote_copy(
            src_ref=src,
            dst_ref=dst,
            send_sem=send_sems.at[i],
            recv_sem=recv_sems.at[i],
            device_id=to,
            device_id_type=MESH,
        )

    def send(*names):
        for name in names:
            sent.append(name)
            messages[name]().start()

    def arrived(*names):
        for name in names:
            messages[name]().wait_recv()

    def query_slot(piece, dc=0):
        half, at = place(TILES, piece)
        return (half * 2 + dc) * 4 + at

    def key_slot(piece):
        chunk, at = place(CHUNKS, piece)
        return chunk * 2 + at

    def back(piece):
        return (-piece[0]) % 4, piece[1]

    here = (0, 0)
    for dx in (1, 3, 2):
        for dz in (0, 1):
            to = query_peer[dx, 0]
            message(f"q{dx}{dz}", qo.at[query_slot((0, dz))], qo.at[query_slot(back((dx, dz)))], to)
            message(f"l{dx}{dz}", ld.at[query_slot((0, dz))], ld.at[query_slot(back((dx, dz)))], to)
            message(f"k{dx}{dz}", kv.at[key_slot((0, dz))], kv.at[key_slot(back((dx, dz)))], key_peer[dx, 0])
    message("q01", qo.at[query_slot(here)], qo.at[query_slot((0, 1))], query_peer[0, 1])
    message("l01", ld.at[query_slot(here)], ld.at[query_slot((0, 1))], query_peer[0, 1])
    message("k01", kv.at[key_slot(here)], kv.at[key_slot((0, 1))], key_peer[0, 1])
    for piece in OFFSETS:
        dx, dz = piece
        message(f"hq{dx}{dz}", qo.at[query_slot(piece)], qo.at[query_slot(piece, 1)], sibling)
        message(f"hl{dx}{dz}", ld.at[query_slot(piece)], ld.at[query_slot(piece, 1)], sibling)
    for half in (0, 1):
        message(f"sq{half}", dq_swap.at[half], dq_swapped.at[half], sibling)
    for i, piece in enumerate(AWAY):
        message(f"dq{piece[0]}{piece[1]}", dq_out.at[i], dq_in.at[i], query_peer[piece])
        message(f"dk{piece[0]}{piece[1]}", dkv_out.at[i], dkv_in.at[i], key_peer[piece if piece == (0, 1) else (piece[0], 0)])

    local = [
        pltpu.make_async_copy(q_hbm, qo.at[0, 0], local_sems.at[0]),
        pltpu.make_async_copy(o_hbm, qo.at[0, 1], local_sems.at[1]),
    ]
    for copy in local:
        copy.start()
    ld[0, 0:1, :] = jnp.concatenate([log_ref[h : h + 1, :] for h in range(HEADS)], axis=1) * LOG2E
    ld[0, 1:2, :] = jnp.concatenate([delta_ref[h : h + 1, :] for h in range(HEADS)], axis=1)
    ld[0, 2:8, :] = jnp.zeros((6, 256), F32)
    for i, (codes, factors) in enumerate(((kcode_ref, kscale_ref), (vcode_ref, vscale_ref))):
        for half in (0, 1):
            rows = pl.ds(half * 128, 128)
            factor = jnp.broadcast_to(factors[half : half + 1, :], (128, 128)).T
            kv[0, i, rows, :] = (codes[rows, :].astype(F32) * factor).astype(BF16)
    diff[...] = lax.broadcasted_iota(jnp.int32, (128, 256), 0) - lax.broadcasted_iota(jnp.int32, (128, 256), 1) % 32
    dq_acc[...] = jnp.zeros_like(dq_acc)
    dk_acc[...] = jnp.zeros_like(dk_acc)
    dv_acc[...] = jnp.zeros_like(dv_acc)
    for copy in local:
        copy.wait()
    pl.semaphore_wait(barrier, len(peers))

    def came(letters, piece):
        dx, dz = back(piece)
        arrived(*(f"{letter}{dx}{dz}" for letter in letters))

    have = set()

    def need(letters, piece):
        name = f"{letters[0]}{piece[0]}{piece[1]}"
        if piece != here and name not in have:
            have.add(name)
            came(letters, piece)

    def hand_over(piece):
        need("ql", piece)
        send(f"hq{piece[0]}{piece[1]}", f"hl{piece[0]}{piece[1]}")

    send("q01", "l01", "k01", "k10", "k30", "q10", "l10", "q30", "l30", "hq00", "hl00", "k20", "q20", "l20")
    hand_over((0, 1))
    send("q11", "l11", "q31", "l31", "q21", "l21")
    hand_over((1, 0))
    hand_over((3, 0))

    def ready(step):
        for piece, at in HAND_OVER.items():
            if at == step:
                hand_over(piece)
        chunk, tile = STEPS[step]
        if all(before[0] != chunk for before in STEPS[:step]):
            for piece in CHUNKS[chunk]:
                need("k", piece)
                if piece == (0, 1):
                    send("k11", "k31", "k21")
        if all(before[1] != tile for before in STEPS[:step]):
            for piece in TILES[tile // 2]:
                if tile % 2:
                    arrived(f"hq{piece[0]}{piece[1]}", f"hl{piece[0]}{piece[1]}")
                else:
                    need("ql", piece)

    def query_part(piece, dc=0):
        half, at = place(TILES, piece)
        return dq_acc[half * 2 + dc, :, at * 256 : (at + 1) * 256]

    def query_sum(piece):
        half, at = place(TILES, piece)
        return query_part(piece) + dq_swapped[half, at].astype(F32)

    def key_part(acc, piece):
        chunk, at = place(CHUNKS, piece)
        return acc[chunk, at * 256 : (at + 1) * 256]

    def key_sums(piece, others):
        total = [key_part(dk_acc, piece), key_part(dv_acc, piece)]
        for other in others:
            arrived(f"dk{other[0]}{other[1]}")
            total = [part + dkv_in[AWAY.index(other), n].astype(F32) for n, part in enumerate(total)]
        return total

    def done(step):
        for chunk in range(4):
            if last_step(0, chunk) == step:
                pieces = [piece for piece in CHUNKS[chunk] if piece[0]]
                for piece in pieces:
                    for n, acc in enumerate((dk_acc, dv_acc)):
                        dkv_out[AWAY.index(piece), n] = key_part(acc, piece).astype(BF16)
                send(*(f"dk{piece[0]}{piece[1]}" for piece in reversed(pieces)))
        if step == CROSS:
            total = key_sums((0, 1), ((1, 1), (3, 1), (2, 1)))
            for n in (0, 1):
                dkv_out[AWAY.index((0, 1)), n] = total[n].astype(BF16)
            send("dk01")
        for half in (0, 1):
            first, second = last_step(1, half * 2), last_step(1, half * 2 + 1)
            if second == step:
                for at, piece in enumerate(TILES[half]):
                    dq_swap[half, at] = query_part(piece, 1).astype(BF16)
                send(f"sq{half}")
            if max(first, second + 1) == step or max(first, second + 1) == len(STEPS) == step + 1:
                arrived(f"sq{half}")
                pieces = [piece for piece in TILES[half] if piece != here]
                for piece in reversed(pieces):
                    dq_out[AWAY.index(piece)] = query_sum(piece).astype(BF16)
                send(*(f"dq{piece[0]}{piece[1]}" for piece in reversed(pieces)))

    def one_step(s, carry):
        for step in range(len(STEPS)):
            pl.when(s == step)(lambda step=step: ready(step))
        c, t = pick([step[0] for step in STEPS], s), pick([step[1] for step in STEPS], s)
        keys = jnp.concatenate([kv[2 * c, 0], kv[2 * c + 1, 0]], axis=0)
        values = jnp.concatenate([kv[2 * c, 1], kv[2 * c + 1, 1]], axis=0)
        starts = []
        for at in (0, 1):
            owner = key_owner(pick([chunk[at][0] for chunk in CHUNKS], c), pick([chunk[at][1] for chunk in CHUNKS], c))
            starts += [kstart_ref[owner * 2], kstart_ref[owner * 2 + 1]]
        offset = diff[...]
        all_q, all_o = [], []
        for at in range(4):
            piece = t * 4 + at
            half = t // 2
            owner = query_owner(
                pick([tile[at][0] for tile in TILES], half), pick([tile[at][1] for tile in TILES], half), t % 2
            )
            first = qstart_ref[owner // 4] + (owner % 4) * 32
            q_rows = jnp.concatenate([qo[piece, 0, :, h * 128 : (h + 1) * 128] for h in range(HEADS)], axis=0)
            o_rows = jnp.concatenate([qo[piece, 1, :, h * 128 : (h + 1) * 128] for h in range(HEADS)], axis=0)
            logs, deltas = ld[piece, 0:1, :], ld[piece, 1:2, :]
            scores = dot(keys, q_rows, 1, 1)
            dprobs = dot(values, o_rows, 1, 1)
            visible = jnp.concatenate([offset <= first - start for start in starts], axis=0)
            attention = jnp.where(visible, jnp.exp2(scores * (SCALE * LOG2E) - logs), 0.0)
            columns = pl.ds(at * 256, 256)
            p_t[:, columns] = attention.astype(BF16)
            ds_t[:, columns] = (attention * (dprobs - deltas)).astype(BF16)
            all_q.append(q_rows)
            all_o.append(o_rows)
        dv_acc[c] += dot(p_t[...], jnp.concatenate(all_o, axis=0), 1, 0)
        dk_acc[c] += dot(ds_t[...], jnp.concatenate(all_q, axis=0), 1, 0)
        dq_acc[t] += dot(keys.T, ds_t[...], 1, 0)
        for step in range(len(STEPS)):
            pl.when(s == step)(lambda step=step: done(step))
        return carry

    lax.fori_loop(0, len(STEPS), one_step, 0)

    keys, values = key_sums(here, ((2, 0), (1, 0), (3, 0), (0, 1)))
    gk_ref[...] = (keys * SCALE).astype(BF16)
    gv_ref[...] = values.astype(BF16)
    total = query_sum(here)
    for i, piece in enumerate(AWAY):
        arrived(f"dq{piece[0]}{piece[1]}")
        total += dq_in[i].astype(F32)
    total = (total * SCALE).T
    for h in range(HEADS):
        gq_ref[:, h * 128 : (h + 1) * 128] = total[h * 32 : (h + 1) * 32].astype(BF16)
    assert sorted(sent) == sorted(messages), set(messages) ^ set(sent)
    for make in messages.values():
        make().wait_send()


def finish(*refs):
    for i in range(3):
        refs[3 + i][...] = refs[i][...]


def local(
    queries, d_out, log_sums, deltas, query_start, key_codes, value_codes, key_scale, value_scale, key_start
):
    vmem = pl.BlockSpec(memory_space=pltpu.VMEM)
    smem = pl.BlockSpec(memory_space=pltpu.SMEM)
    anywhere = pl.BlockSpec(memory_space=pl.ANY)
    piece = (128, 256)
    outs = (
        jax.ShapeDtypeStruct((32, 1024), BF16),
        jax.ShapeDtypeStruct((256, 128), BF16),
        jax.ShapeDtypeStruct((256, 128), BF16),
    )
    grads = pl.pallas_call(
        kernel,
        out_shape=outs,
        in_specs=[anywhere, anywhere, vmem, vmem, smem, vmem, vmem, vmem, vmem, smem],
        out_specs=[vmem, vmem, vmem],
        scratch_shapes=[
            pltpu.VMEM((16, 2, 32, 1024), BF16),
            pltpu.VMEM((16, 8, 256), F32),
            pltpu.VMEM((8, 2, 256, 128), BF16),
            pltpu.VMEM((4, 128, 1024), F32),
            pltpu.VMEM((4, 512, 128), F32),
            pltpu.VMEM((4, 512, 128), F32),
            pltpu.VMEM((512, 1024), BF16),
            pltpu.VMEM((512, 1024), BF16),
            pltpu.VMEM((128, 256), jnp.int32),
            pltpu.VMEM((2, 4, *piece), BF16),
            pltpu.VMEM((2, 4, *piece), BF16),
            pltpu.VMEM((7, *piece), BF16),
            pltpu.VMEM((7, *piece), BF16),
            pltpu.VMEM((7, 2, 256, 128), BF16),
            pltpu.VMEM((7, 2, 256, 128), BF16),
            pltpu.SemaphoreType.DMA((N_MESSAGES,)),
            pltpu.SemaphoreType.DMA((N_MESSAGES,)),
            pltpu.SemaphoreType.DMA((2,)),
        ],
        compiler_params=pltpu.CompilerParams(
            collective_id=0, has_side_effects=True, vmem_limit_bytes=60 << 20
        ),
        name="fused",
    )(
        queries,
        d_out,
        log_sums,
        deltas,
        query_start,
        key_codes,
        value_codes,
        key_scale.reshape(2, 128),
        value_scale.reshape(2, 128),
        key_start,
    )
    return pl.pallas_call(finish, out_shape=outs, in_specs=[vmem] * 3, out_specs=[vmem] * 3, name="finish")(*grads)


def solution(mesh):
    placed = (
        P(("pb", "ka"), None),
        P(("pb", "ka"), None),
        P(None, ("pb", "ka")),
        P(None, ("pb", "ka")),
        P("pb"),
        P(("ka", "pb"), None),
        P(("ka", "pb"), None),
        P(("ka", "pb")),
        P(("ka", "pb")),
        P("ka"),
    )
    return jax.shard_map(
        local,
        mesh=mesh,
        in_specs=placed,
        out_specs=(P(("pb", "ka"), None), P(("ka", "pb"), None), P(("ka", "pb"), None)),
        check_vma=False,
    )
```

```python
import math

import jax
import jax.numpy as jnp
from jax import lax
from jax.experimental import pallas as pl
from jax.experimental.pallas import tpu as pltpu
from jax.sharding import PartitionSpec as P

HEADS = 8
HEAD_DIM = 128
SCALE = 1.0 / math.sqrt(HEAD_DIM)
LOG2E = math.log2(math.e)
MESH = pl.DeviceIdType.MESH
BF16 = jnp.bfloat16
FAR = 1 << 15
F32 = jnp.float32

TILES = (
    ((0, 0, 0), (1, 0, 0), (3, 0, 0), (0, 1, 0)),
    ((0, 0, 1), (1, 0, 1), (3, 0, 1), (0, 1, 1)),
    ((2, 0, 0), (1, 1, 0), (3, 1, 0), (2, 1, 0)),
    ((2, 0, 1), (1, 1, 1), (3, 1, 1), (2, 1, 1)),
)
CHUNKS = (((0, 0), (0, 1)), ((1, 0), (3, 0)), ((1, 1), (3, 1)), ((2, 0), (2, 1)))
STEPS = (
    (1, 0), (0, 0), (1, 1), (0, 1), (2, 0), (2, 1), (2, 2), (3, 0),
    (2, 3), (3, 1), (3, 3), (3, 2), (0, 3), (1, 3), (0, 2), (1, 2),
)
CROSS = 14
HAND_OVER = {(2, 0): 4, (1, 1): 5, (3, 1): 5, (2, 1): 6}
OFFSETS = tuple((d, dz) for dz in (0, 1) for d in (0, 1, 3, 2))
AWAY = OFFSETS[1:]
N_MESSAGES = 66


def place(groups, piece):
    for i, group in enumerate(groups):
        if piece in group:
            return i, group.index(piece)


def last_step(column, index):
    return max(i for i, step in enumerate(STEPS) if step[column] == index)


def dot(a, b, ca, cb):
    return lax.dot_general(a, b, (((ca,), (cb,)), ((), ())), preferred_element_type=F32)


def pick(table, s):
    value = jnp.int32(table[0])
    for i, entry in enumerate(table[1:], 1):
        value = jnp.where(s == i, jnp.int32(entry), value)
    return value


def flip(bit, by):
    return bit + by - 2 * bit * by


def kernel(
    q_hbm,
    o_hbm,
    log_ref,
    delta_ref,
    qstart_ref,
    kcode_ref,
    vcode_ref,
    kscale_ref,
    vscale_ref,
    kstart_ref,
    gq_ref,
    gk_ref,
    gv_ref,
    qo,
    ld,
    kv,
    dq_acc,
    dk_acc,
    dv_acc,
    p_t,
    ds_t,
    diff,
    dq_swap,
    dq_swapped,
    dq_out,
    dq_in,
    dkv_out,
    dkv_in,
    send_sems,
    recv_sems,
    local_sems,
):
    g = lax.axis_index("pb")
    k = lax.axis_index("ka")
    zh, y = g // 4, g % 4
    zl, x, core = k // 8, (k // 2) % 4, k % 2

    def query_owner(dx, dz, dc=0):
        return flip(zl, dz) * 8 + ((x + dx) % 4) * 2 + flip(core, dc)

    def key_owner(dy, dz):
        return flip(zh, dz) * 4 + (y + dy) % 4

    sibling = (g, query_owner(0, 0, 1))
    query_peer = {piece: (g, query_owner(*piece)) for piece in AWAY}
    key_peer = {piece: (key_owner(*piece), k) for piece in AWAY if 0 in piece}
    peers = [sibling, *query_peer.values(), *key_peer.values()]
    barrier = pltpu.get_barrier_semaphore()
    for to in peers:
        pl.semaphore_signal(barrier, inc=1, device_id=to, device_id_type=MESH)

    messages, sent = {}, []

    def message(name, src, dst, to):
        i = len(messages)
        assert name not in messages and i < N_MESSAGES
        messages[name] = lambda: pltpu.make_async_remote_copy(
            src_ref=src,
            dst_ref=dst,
            send_sem=send_sems.at[i],
            recv_sem=recv_sems.at[i],
            device_id=to,
            device_id_type=MESH,
        )

    def send(*names):
        for name in names:
            sent.append(name)
            messages[name]().start()

    def arrived(*names):
        for name in names:
            messages[name]().wait_recv()

    def query_slot(piece, dc=0):
        tile, at = place(TILES, (*piece, dc))
        return tile * 4 + at

    def key_slot(piece):
        chunk, at = place(CHUNKS, piece)
        return chunk * 2 + at

    def back(piece):
        return (-piece[0]) % 4, piece[1]

    here = (0, 0)
    for dx in (1, 3, 2):
        for dz in (0, 1):
            to = query_peer[dx, 0]
            message(f"q{dx}{dz}", qo.at[query_slot((0, dz))], qo.at[query_slot(back((dx, dz)))], to)
            message(f"l{dx}{dz}", ld.at[query_slot((0, dz))], ld.at[query_slot(back((dx, dz)))], to)
            message(f"k{dx}{dz}", kv.at[key_slot((0, dz))], kv.at[key_slot(back((dx, dz)))], key_peer[dx, 0])
    message("q01", qo.at[query_slot(here)], qo.at[query_slot((0, 1))], query_peer[0, 1])
    message("l01", ld.at[query_slot(here)], ld.at[query_slot((0, 1))], query_peer[0, 1])
    message("k01", kv.at[key_slot(here)], kv.at[key_slot((0, 1))], key_peer[0, 1])
    for piece in OFFSETS:
        dx, dz = piece
        message(f"hq{dx}{dz}", qo.at[query_slot(piece)], qo.at[query_slot(piece, 1)], sibling)
        message(f"hl{dx}{dz}", ld.at[query_slot(piece)], ld.at[query_slot(piece, 1)], sibling)
        i = OFFSETS.index(piece)
        message(f"sq{dx}{dz}", dq_swap.at[i], dq_swapped.at[i], sibling)
    for i, piece in enumerate(AWAY):
        message(f"dq{piece[0]}{piece[1]}", dq_out.at[i], dq_in.at[i], query_peer[piece])
        message(f"dk{piece[0]}{piece[1]}", dkv_out.at[i], dkv_in.at[i], key_peer[piece if piece == (0, 1) else (piece[0], 0)])

    local = [
        pltpu.make_async_copy(q_hbm, qo.at[0, 0], local_sems.at[0]),
        pltpu.make_async_copy(o_hbm, qo.at[0, 1], local_sems.at[1]),
    ]
    for copy in local:
        copy.start()
    ld[0, 0:1, :] = jnp.concatenate([log_ref[h : h + 1, :] for h in range(HEADS)], axis=1) * LOG2E
    ld[0, 1:2, :] = jnp.concatenate([delta_ref[h : h + 1, :] for h in range(HEADS)], axis=1)
    ld[0, 2:8, :] = jnp.zeros((6, 256), F32)
    for i, (codes, factors) in enumerate(((kcode_ref, kscale_ref), (vcode_ref, vscale_ref))):
        for half in (0, 1):
            rows = pl.ds(half * 128, 128)
            factor = jnp.broadcast_to(factors[half : half + 1, :], (128, 128)).T
            kv[0, i, rows, :] = (codes[rows, :].astype(F32) * factor).astype(BF16)
    steps_apart = lax.broadcasted_iota(jnp.int32, (128, 256), 0) - lax.broadcasted_iota(jnp.int32, (128, 256), 1) % 32
    diff[...] = (steps_apart * FAR).astype(F32)
    dq_acc[...] = jnp.zeros_like(dq_acc)
    dk_acc[...] = jnp.zeros_like(dk_acc)
    dv_acc[...] = jnp.zeros_like(dv_acc)
    for copy in local:
        copy.wait()
    pl.semaphore_wait(barrier, len(peers))

    def came(letters, piece):
        dx, dz = back(piece)
        arrived(*(f"{letter}{dx}{dz}" for letter in letters))

    have = set()

    def need(letters, piece):
        name = f"{letters[0]}{piece[0]}{piece[1]}"
        if piece != here and name not in have:
            have.add(name)
            came(letters, piece)

    def hand_over(piece):
        need("ql", piece)
        send(f"hq{piece[0]}{piece[1]}", f"hl{piece[0]}{piece[1]}")

    send("q01", "l01", "k01", "k10", "k30", "q10", "l10", "q30", "l30", "hq00", "hl00", "k20", "q20", "l20")
    hand_over((0, 1))
    send("q11", "l11", "q31", "l31", "q21", "l21")
    hand_over((1, 0))
    hand_over((3, 0))

    def ready(step):
        for piece, at in HAND_OVER.items():
            if at == step:
                hand_over(piece)
        chunk, tile = STEPS[step]
        if all(before[0] != chunk for before in STEPS[:step]):
            for piece in CHUNKS[chunk]:
                need("k", piece)
                if piece == (0, 1):
                    send("k11", "k31", "k21")
        if all(before[1] != tile for before in STEPS[:step]):
            for dx, dz, dc in TILES[tile]:
                if dc:
                    arrived(f"hq{dx}{dz}", f"hl{dx}{dz}")
                else:
                    need("ql", (dx, dz))

    def query_part(piece, dc=0):
        tile, at = place(TILES, (*piece, dc))
        return dq_acc[tile, :, at * 256 : (at + 1) * 256]

    def query_sum(piece):
        arrived(f"sq{piece[0]}{piece[1]}")
        return query_part(piece) + dq_swapped[OFFSETS.index(piece)].astype(F32)

    def swaps(step):
        return [(dx, dz) for dx, dz, dc in TILES[STEPS[step][1]] if dc and last_step(1, STEPS[step][1]) == step]

    def sums(step):
        for piece in AWAY:
            first, second = (last_step(1, place(TILES, (*piece, dc))[0]) for dc in (0, 1))
            at = max(first, second + 1)
            if at == step:
                yield piece

    def key_part(acc, piece):
        chunk, at = place(CHUNKS, piece)
        return acc[chunk, at * 256 : (at + 1) * 256]

    def key_sums(piece, others):
        total = [key_part(dk_acc, piece), key_part(dv_acc, piece)]
        for other in others:
            arrived(f"dk{other[0]}{other[1]}")
            total = [part + dkv_in[AWAY.index(other), n].astype(F32) for n, part in enumerate(total)]
        return total

    def done(step):
        for chunk in range(4):
            if last_step(0, chunk) == step:
                pieces = [piece for piece in CHUNKS[chunk] if piece[0]]
                for piece in pieces:
                    for n, acc in enumerate((dk_acc, dv_acc)):
                        dkv_out[AWAY.index(piece), n] = key_part(acc, piece).astype(BF16)
                send(*(f"dk{piece[0]}{piece[1]}" for piece in reversed(pieces)))
        if step == CROSS:
            total = key_sums((0, 1), ((1, 1), (3, 1), (2, 1)))
            for n in (0, 1):
                dkv_out[AWAY.index((0, 1)), n] = total[n].astype(BF16)
            send("dk01")
        for piece in swaps(step):
            dq_swap[OFFSETS.index(piece)] = query_part(piece, 1).astype(BF16)
        send(*(f"sq{dx}{dz}" for dx, dz in swaps(step)))
        hand_in(step)

    def hand_in(step):
        ready_now = sorted(sums(step), key=lambda piece: (-piece[1], -(piece[0] % 2), piece))
        for piece in ready_now:
            dq_out[AWAY.index(piece)] = query_sum(piece).astype(BF16)
            send(f"dq{piece[0]}{piece[1]}")

    def one_step(s, carry):
        for step in range(len(STEPS)):
            pl.when(s == step)(lambda step=step: ready(step))
        c, t = pick([step[0] for step in STEPS], s), pick([step[1] for step in STEPS], s)
        keys = jnp.concatenate([kv[2 * c, 0], kv[2 * c + 1, 0]], axis=0)
        values = jnp.concatenate([kv[2 * c, 1], kv[2 * c + 1, 1]], axis=0)
        starts = []
        for at in (0, 1):
            owner = key_owner(pick([chunk[at][0] for chunk in CHUNKS], c), pick([chunk[at][1] for chunk in CHUNKS], c))
            starts += [kstart_ref[owner * 2], kstart_ref[owner * 2 + 1]]
        offset = diff[...]
        all_q, all_o = [], []
        for at in range(4):
            piece = t * 4 + at
            owner = query_owner(*(pick([tile[at][n] for tile in TILES], t) for n in range(3)))
            first = qstart_ref[owner // 4] + (owner % 4) * 32
            q_rows = jnp.concatenate([qo[piece, 0, :, h * 128 : (h + 1) * 128] for h in range(HEADS)], axis=0)
            o_rows = jnp.concatenate([qo[piece, 1, :, h * 128 : (h + 1) * 128] for h in range(HEADS)], axis=0)
            logs, deltas = ld[piece, 0:1, :], ld[piece, 1:2, :]
            scores = dot(keys, q_rows, 1, 1)
            dprobs = dot(values, o_rows, 1, 1)
            unseen = jnp.concatenate([jnp.minimum(((first - start) * FAR).astype(F32) - offset, 0.0) for start in starts], axis=0)
            attention = jnp.exp2(scores * (SCALE * LOG2E) - logs + unseen)
            columns = pl.ds(at * 256, 256)
            p_t[:, columns] = attention.astype(BF16)
            ds_t[:, columns] = (attention * (dprobs - deltas)).astype(BF16)
            all_q.append(q_rows)
            all_o.append(o_rows)
        dv_acc[c] += dot(p_t[...], jnp.concatenate(all_o, axis=0), 1, 0)
        dk_acc[c] += dot(ds_t[...], jnp.concatenate(all_q, axis=0), 1, 0)
        dq_acc[t] += dot(keys.T, ds_t[...], 1, 0)
        for step in range(len(STEPS)):
            pl.when(s == step)(lambda step=step: done(step))
        return carry

    lax.fori_loop(0, len(STEPS), one_step, 0)

    hand_in(len(STEPS))
    keys, values = key_sums(here, ((2, 0), (1, 0), (3, 0), (0, 1)))
    gk_ref[...] = (keys * SCALE).astype(BF16)
    gv_ref[...] = values.astype(BF16)
    total = query_sum(here)
    for i, piece in enumerate(AWAY):
        arrived(f"dq{piece[0]}{piece[1]}")
        total += dq_in[i].astype(F32)
    total = (total * SCALE).T
    for h in range(HEADS):
        gq_ref[:, h * 128 : (h + 1) * 128] = total[h * 32 : (h + 1) * 32].astype(BF16)
    assert sorted(sent) == sorted(messages), set(messages) ^ set(sent)
    for make in messages.values():
        make().wait_send()


def finish(*refs):
    for i in range(3):
        refs[3 + i][...] = refs[i][...]


def local(
    queries, d_out, log_sums, deltas, query_start, key_codes, value_codes, key_scale, value_scale, key_start
):
    vmem = pl.BlockSpec(memory_space=pltpu.VMEM)
    smem = pl.BlockSpec(memory_space=pltpu.SMEM)
    anywhere = pl.BlockSpec(memory_space=pl.ANY)
    piece = (128, 256)
    outs = (
        jax.ShapeDtypeStruct((32, 1024), BF16),
        jax.ShapeDtypeStruct((256, 128), BF16),
        jax.ShapeDtypeStruct((256, 128), BF16),
    )
    grads = pl.pallas_call(
        kernel,
        out_shape=outs,
        in_specs=[anywhere, anywhere, vmem, vmem, smem, vmem, vmem, vmem, vmem, smem],
        out_specs=[vmem, vmem, vmem],
        scratch_shapes=[
            pltpu.VMEM((16, 2, 32, 1024), BF16),
            pltpu.VMEM((16, 8, 256), F32),
            pltpu.VMEM((8, 2, 256, 128), BF16),
            pltpu.VMEM((4, 128, 1024), F32),
            pltpu.VMEM((4, 512, 128), F32),
            pltpu.VMEM((4, 512, 128), F32),
            pltpu.VMEM((512, 1024), BF16),
            pltpu.VMEM((512, 1024), BF16),
            pltpu.VMEM((128, 256), F32),
            pltpu.VMEM((8, *piece), BF16),
            pltpu.VMEM((8, *piece), BF16),
            pltpu.VMEM((7, *piece), BF16),
            pltpu.VMEM((7, *piece), BF16),
            pltpu.VMEM((7, 2, 256, 128), BF16),
            pltpu.VMEM((7, 2, 256, 128), BF16),
            pltpu.SemaphoreType.DMA((N_MESSAGES,)),
            pltpu.SemaphoreType.DMA((N_MESSAGES,)),
            pltpu.SemaphoreType.DMA((2,)),
        ],
        compiler_params=pltpu.CompilerParams(
            collective_id=0, has_side_effects=True, vmem_limit_bytes=60 << 20
        ),
        name="fused",
    )(
        queries,
        d_out,
        log_sums,
        deltas,
        query_start,
        key_codes,
        value_codes,
        key_scale.reshape(2, 128),
        value_scale.reshape(2, 128),
        key_start,
    )
    return pl.pallas_call(finish, out_shape=outs, in_specs=[vmem] * 3, out_specs=[vmem] * 3, name="finish")(*grads)


def solution(mesh):
    placed = (
        P(("pb", "ka"), None),
        P(("pb", "ka"), None),
        P(None, ("pb", "ka")),
        P(None, ("pb", "ka")),
        P("pb"),
        P(("ka", "pb"), None),
        P(("ka", "pb"), None),
        P(("ka", "pb")),
        P(("ka", "pb")),
        P("ka"),
    )
    return jax.shard_map(
        local,
        mesh=mesh,
        in_specs=placed,
        out_specs=(P(("pb", "ka"), None), P(("ka", "pb"), None), P(("ka", "pb"), None)),
        check_vma=False,
    )
```

```python
import math

import jax
import jax.numpy as jnp
from jax import lax
from jax.experimental import pallas as pl
from jax.experimental.pallas import tpu as pltpu
from jax.sharding import PartitionSpec as P

HEADS = 8
HEAD_DIM = 128
SCALE = 1.0 / math.sqrt(HEAD_DIM)
LOG2E = math.log2(math.e)
MESH = pl.DeviceIdType.MESH
BF16 = jnp.bfloat16
FAR = 1 << 15
F32 = jnp.float32

TILES = (
    ((0, 0, 0), (1, 0, 0), (3, 0, 0), (0, 1, 0)),
    ((0, 0, 1), (1, 0, 1), (3, 0, 1), (0, 1, 1)),
    ((2, 0, 0), (1, 1, 0), (3, 1, 0), (2, 1, 0)),
    ((2, 0, 1), (1, 1, 1), (3, 1, 1), (2, 1, 1)),
)
CHUNKS = (((0, 0), (0, 1)), ((1, 0), (3, 0)), ((1, 1), (3, 1)), ((2, 0), (2, 1)))
STEPS = (
    (0, 0), (0, 1), (1, 1), (2, 0), (2, 1), (2, 2), (3, 0), (2, 3),
    (3, 1), (3, 3), (3, 2), (0, 3), (1, 3), (0, 2), (1, 2), (1, 0),
)
CROSS = 14
HAND_OVER = {(2, 0): 3, (1, 1): 4, (3, 1): 4, (2, 1): 5}
OFFSETS = tuple((d, dz) for dz in (0, 1) for d in (0, 1, 3, 2))
AWAY = OFFSETS[1:]
N_MESSAGES = 66


def place(groups, piece):
    for i, group in enumerate(groups):
        if piece in group:
            return i, group.index(piece)


def last_step(column, index):
    return max(i for i, step in enumerate(STEPS) if step[column] == index)


def dot(a, b, ca, cb):
    return lax.dot_general(a, b, (((ca,), (cb,)), ((), ())), preferred_element_type=F32)


def pick(table, s):
    value = jnp.int32(table[0])
    for i, entry in enumerate(table[1:], 1):
        value = jnp.where(s == i, jnp.int32(entry), value)
    return value


def flip(bit, by):
    return bit + by - 2 * bit * by


def kernel(
    q_hbm,
    o_hbm,
    log_ref,
    delta_ref,
    qstart_ref,
    kcode_ref,
    vcode_ref,
    kscale_ref,
    vscale_ref,
    kstart_ref,
    gq_ref,
    gk_ref,
    gv_ref,
    qo,
    ld,
    kv,
    dq_acc,
    dk_acc,
    dv_acc,
    p_t,
    ds_t,
    diff,
    dq_swap,
    dq_swapped,
    dq_out,
    dq_in,
    dkv_out,
    dkv_in,
    send_sems,
    recv_sems,
    local_sems,
):
    g = lax.axis_index("pb")
    k = lax.axis_index("ka")
    zh, y = g // 4, g % 4
    zl, x, core = k // 8, (k // 2) % 4, k % 2

    def query_owner(dx, dz, dc=0):
        return flip(zl, dz) * 8 + ((x + dx) % 4) * 2 + flip(core, dc)

    def key_owner(dy, dz):
        return flip(zh, dz) * 4 + (y + dy) % 4

    sibling = (g, query_owner(0, 0, 1))
    query_peer = {piece: (g, query_owner(*piece)) for piece in AWAY if 0 in piece}
    key_peer = {piece: (key_owner(*piece), k) for piece in AWAY if 0 in piece}
    peers = [sibling, *query_peer.values(), *key_peer.values()]
    barrier = pltpu.get_barrier_semaphore()
    for to in peers:
        pl.semaphore_signal(barrier, inc=1, device_id=to, device_id_type=MESH)

    messages, sent = {}, []

    def message(name, src, dst, to):
        i = len(messages)
        assert name not in messages and i < N_MESSAGES
        messages[name] = lambda: pltpu.make_async_remote_copy(
            src_ref=src,
            dst_ref=dst,
            send_sem=send_sems.at[i],
            recv_sem=recv_sems.at[i],
            device_id=to,
            device_id_type=MESH,
        )

    def send(*names):
        for name in names:
            sent.append(name)
            messages[name]().start()

    def arrived(*names):
        for name in names:
            messages[name]().wait_recv()

    def query_slot(piece, dc=0):
        tile, at = place(TILES, (*piece, dc))
        return tile * 4 + at

    def key_slot(piece):
        chunk, at = place(CHUNKS, piece)
        return chunk * 2 + at

    def back(piece):
        return (-piece[0]) % 4, piece[1]

    here = (0, 0)
    for dx in (1, 3, 2):
        for dz in (0, 1):
            to = query_peer[dx, 0]
            message(f"q{dx}{dz}", qo.at[query_slot((0, dz))], qo.at[query_slot(back((dx, dz)))], to)
            message(f"l{dx}{dz}", ld.at[query_slot((0, dz))], ld.at[query_slot(back((dx, dz)))], to)
            message(f"k{dx}{dz}", kv.at[key_slot((0, dz))], kv.at[key_slot(back((dx, dz)))], key_peer[dx, 0])
    message("q01", qo.at[query_slot(here)], qo.at[query_slot((0, 1))], query_peer[0, 1])
    message("l01", ld.at[query_slot(here)], ld.at[query_slot((0, 1))], query_peer[0, 1])
    message("k01", kv.at[key_slot(here)], kv.at[key_slot((0, 1))], key_peer[0, 1])
    for piece in OFFSETS:
        dx, dz = piece
        message(f"hq{dx}{dz}", qo.at[query_slot(piece)], qo.at[query_slot(piece, 1)], sibling)
        message(f"hl{dx}{dz}", ld.at[query_slot(piece)], ld.at[query_slot(piece, 1)], sibling)
        i = OFFSETS.index(piece)
        message(f"sq{dx}{dz}", dq_swap.at[i], dq_swapped.at[i], sibling)
    for i, piece in enumerate(AWAY):
        message(f"dq{piece[0]}{piece[1]}", dq_out.at[i], dq_in.at[i], query_peer[piece if piece == (0, 1) else (piece[0], 0)])
        message(f"dk{piece[0]}{piece[1]}", dkv_out.at[i], dkv_in.at[i], key_peer[piece if piece == (0, 1) else (piece[0], 0)])

    local = [
        pltpu.make_async_copy(q_hbm, qo.at[0, 0], local_sems.at[0]),
        pltpu.make_async_copy(o_hbm, qo.at[0, 1], local_sems.at[1]),
    ]
    for copy in local:
        copy.start()
    ld[0, 0:1, :] = jnp.concatenate([log_ref[h : h + 1, :] for h in range(HEADS)], axis=1) * LOG2E
    ld[0, 1:2, :] = jnp.concatenate([delta_ref[h : h + 1, :] for h in range(HEADS)], axis=1)
    ld[0, 2:8, :] = jnp.zeros((6, 256), F32)
    for i, (codes, factors) in enumerate(((kcode_ref, kscale_ref), (vcode_ref, vscale_ref))):
        for half in (0, 1):
            rows = pl.ds(half * 128, 128)
            factor = jnp.broadcast_to(factors[half : half + 1, :], (128, 128)).T
            kv[0, i, rows, :] = (codes[rows, :].astype(F32) * factor).astype(BF16)
    steps_apart = lax.broadcasted_iota(jnp.int32, (128, 256), 0) - lax.broadcasted_iota(jnp.int32, (128, 256), 1) % 32
    diff[...] = (steps_apart * FAR).astype(F32)
    dq_acc[...] = jnp.zeros_like(dq_acc)
    dk_acc[...] = jnp.zeros_like(dk_acc)
    dv_acc[...] = jnp.zeros_like(dv_acc)
    for copy in local:
        copy.wait()
    pl.semaphore_wait(barrier, len(peers))

    def came(letters, piece):
        dx, dz = back(piece)
        arrived(*(f"{letter}{dx}{dz}" for letter in letters))

    have = set()

    def need(letters, piece):
        name = f"{letters[0]}{piece[0]}{piece[1]}"
        if piece != here and name not in have:
            have.add(name)
            came(letters, piece)

    def hand_over(piece):
        need("ql", piece)
        send(f"hq{piece[0]}{piece[1]}", f"hl{piece[0]}{piece[1]}")

    send("k01", "q01", "l01", "k10", "k30", "q10", "l10", "q30", "l30", "hq00", "hl00", "k20", "q20", "l20")
    hand_over((0, 1))
    send("q11", "l11", "q31", "l31", "q21", "l21")
    hand_over((1, 0))
    hand_over((3, 0))
    need("k", (0, 1))
    send("k11", "k31", "k21")

    def ready(step):
        for piece, at in HAND_OVER.items():
            if at == step:
                hand_over(piece)
        chunk, tile = STEPS[step]
        if all(before[0] != chunk for before in STEPS[:step]):
            for piece in CHUNKS[chunk]:
                need("k", piece)
        if all(before[1] != tile for before in STEPS[:step]):
            for dx, dz, dc in TILES[tile]:
                if dc:
                    arrived(f"hq{dx}{dz}", f"hl{dx}{dz}")
                else:
                    need("ql", (dx, dz))

    def query_part(piece, dc=0):
        tile, at = place(TILES, (*piece, dc))
        return dq_acc[tile, :, at * 256 : (at + 1) * 256]

    def query_sum(piece):
        arrived(f"sq{piece[0]}{piece[1]}")
        return query_part(piece) + dq_swapped[OFFSETS.index(piece)].astype(F32)

    def swaps(step):
        return [(dx, dz) for dx, dz, dc in TILES[STEPS[step][1]] if dc and last_step(1, STEPS[step][1]) == step]

    def sums(step):
        for piece in AWAY:
            first, second = (last_step(1, place(TILES, (*piece, dc))[0]) for dc in (0, 1))
            at = max(first, second + 1)
            if at == step:
                yield piece

    def key_part(acc, piece):
        chunk, at = place(CHUNKS, piece)
        return acc[chunk, at * 256 : (at + 1) * 256]

    def key_sums(piece, others):
        total = [key_part(dk_acc, piece), key_part(dv_acc, piece)]
        for other in others:
            arrived(f"dk{other[0]}{other[1]}")
            total = [part + dkv_in[AWAY.index(other), n].astype(F32) for n, part in enumerate(total)]
        return total

    def done(step):
        for chunk in range(4):
            if last_step(0, chunk) == step:
                pieces = [piece for piece in CHUNKS[chunk] if piece[0]]
                for piece in pieces:
                    for n, acc in enumerate((dk_acc, dv_acc)):
                        dkv_out[AWAY.index(piece), n] = key_part(acc, piece).astype(BF16)
                send(*(f"dk{piece[0]}{piece[1]}" for piece in reversed(pieces)))
        for piece in swaps(step):
            dq_swap[OFFSETS.index(piece)] = query_part(piece, 1).astype(BF16)
        send(*(f"sq{dx}{dz}" for dx, dz in swaps(step)))
        if step == CROSS:
            total = key_sums((0, 1), ((1, 1), (3, 1), (2, 1)))
            for n in (0, 1):
                dkv_out[AWAY.index((0, 1)), n] = total[n].astype(BF16)
            send("dk01")
        hand_in(step)

    def hand_in(step):
        ready_now = sorted(sums(step), key=lambda piece: (-piece[1], -(piece[0] % 2), piece))
        for piece in ready_now:
            if piece == (0, 1):
                continue
            dq_out[AWAY.index(piece)] = query_sum(piece).astype(BF16)
            send(f"dq{piece[0]}{piece[1]}")

    def one_step(s, carry):
        for step in range(len(STEPS)):
            pl.when(s == step)(lambda step=step: ready(step))
        c, t = pick([step[0] for step in STEPS], s), pick([step[1] for step in STEPS], s)
        keys = jnp.concatenate([kv[2 * c, 0], kv[2 * c + 1, 0]], axis=0)
        values = jnp.concatenate([kv[2 * c, 1], kv[2 * c + 1, 1]], axis=0)
        starts = []
        for at in (0, 1):
            owner = key_owner(pick([chunk[at][0] for chunk in CHUNKS], c), pick([chunk[at][1] for chunk in CHUNKS], c))
            starts += [kstart_ref[owner * 2], kstart_ref[owner * 2 + 1]]
        offset = diff[...]
        all_q, all_o = [], []
        for at in range(4):
            piece = t * 4 + at
            owner = query_owner(*(pick([tile[at][n] for tile in TILES], t) for n in range(3)))
            first = qstart_ref[owner // 4] + (owner % 4) * 32
            q_rows = jnp.concatenate([qo[piece, 0, :, h * 128 : (h + 1) * 128] for h in range(HEADS)], axis=0)
            o_rows = jnp.concatenate([qo[piece, 1, :, h * 128 : (h + 1) * 128] for h in range(HEADS)], axis=0)
            logs, deltas = ld[piece, 0:1, :], ld[piece, 1:2, :]
            scores = dot(keys, q_rows, 1, 1)
            dprobs = dot(values, o_rows, 1, 1)
            unseen = jnp.concatenate([jnp.minimum(((first - start) * FAR).astype(F32) - offset, 0.0) for start in starts], axis=0)
            attention = jnp.exp2(scores * (SCALE * LOG2E) - logs + unseen)
            columns = pl.ds(at * 256, 256)
            p_t[:, columns] = attention.astype(BF16)
            ds_t[:, columns] = (attention * (dprobs - deltas)).astype(BF16)
            all_q.append(q_rows)
            all_o.append(o_rows)
        dv_acc[c] += dot(p_t[...], jnp.concatenate(all_o, axis=0), 1, 0)
        dk_acc[c] += dot(ds_t[...], jnp.concatenate(all_q, axis=0), 1, 0)
        dq_acc[t] += dot(keys.T, ds_t[...], 1, 0)
        for step in range(len(STEPS)):
            pl.when(s == step)(lambda step=step: done(step))
        return carry

    lax.fori_loop(0, len(STEPS), one_step, 0)

    hand_in(len(STEPS))
    total = query_sum((0, 1))
    for piece in ((1, 1), (3, 1), (2, 1)):
        arrived(f"dq{piece[0]}{piece[1]}")
        total += dq_in[AWAY.index(piece)].astype(F32)
    dq_out[AWAY.index((0, 1))] = total.astype(BF16)
    send("dq01")
    keys, values = key_sums(here, ((2, 0), (1, 0), (3, 0), (0, 1)))
    gk_ref[...] = (keys * SCALE).astype(BF16)
    gv_ref[...] = values.astype(BF16)
    total = query_sum(here)
    for piece in ((1, 0), (3, 0), (2, 0), (0, 1)):
        arrived(f"dq{piece[0]}{piece[1]}")
        total += dq_in[AWAY.index(piece)].astype(F32)
    total = (total * SCALE).T
    for h in range(HEADS):
        gq_ref[:, h * 128 : (h + 1) * 128] = total[h * 32 : (h + 1) * 32].astype(BF16)
    assert sorted(sent) == sorted(messages), set(messages) ^ set(sent)
    for make in messages.values():
        make().wait_send()


def finish(*refs):
    for i in range(3):
        refs[3 + i][...] = refs[i][...]


def local(
    queries, d_out, log_sums, deltas, query_start, key_codes, value_codes, key_scale, value_scale, key_start
):
    vmem = pl.BlockSpec(memory_space=pltpu.VMEM)
    smem = pl.BlockSpec(memory_space=pltpu.SMEM)
    anywhere = pl.BlockSpec(memory_space=pl.ANY)
    piece = (128, 256)
    outs = (
        jax.ShapeDtypeStruct((32, 1024), BF16),
        jax.ShapeDtypeStruct((256, 128), BF16),
        jax.ShapeDtypeStruct((256, 128), BF16),
    )
    grads = pl.pallas_call(
        kernel,
        out_shape=outs,
        in_specs=[anywhere, anywhere, vmem, vmem, smem, vmem, vmem, vmem, vmem, smem],
        out_specs=[vmem, vmem, vmem],
        scratch_shapes=[
            pltpu.VMEM((16, 2, 32, 1024), BF16),
            pltpu.VMEM((16, 8, 256), F32),
            pltpu.VMEM((8, 2, 256, 128), BF16),
            pltpu.VMEM((4, 128, 1024), F32),
            pltpu.VMEM((4, 512, 128), F32),
            pltpu.VMEM((4, 512, 128), F32),
            pltpu.VMEM((512, 1024), BF16),
            pltpu.VMEM((512, 1024), BF16),
            pltpu.VMEM((128, 256), F32),
            pltpu.VMEM((8, *piece), BF16),
            pltpu.VMEM((8, *piece), BF16),
            pltpu.VMEM((7, *piece), BF16),
            pltpu.VMEM((7, *piece), BF16),
            pltpu.VMEM((7, 2, 256, 128), BF16),
            pltpu.VMEM((7, 2, 256, 128), BF16),
            pltpu.SemaphoreType.DMA((N_MESSAGES,)),
            pltpu.SemaphoreType.DMA((N_MESSAGES,)),
            pltpu.SemaphoreType.DMA((2,)),
        ],
        compiler_params=pltpu.CompilerParams(
            collective_id=0, has_side_effects=True, vmem_limit_bytes=60 << 20
        ),
        name="fused",
    )(
        queries,
        d_out,
        log_sums,
        deltas,
        query_start,
        key_codes,
        value_codes,
        key_scale.reshape(2, 128),
        value_scale.reshape(2, 128),
        key_start,
    )
    return pl.pallas_call(finish, out_shape=outs, in_specs=[vmem] * 3, out_specs=[vmem] * 3, name="finish")(*grads)


def solution(mesh):
    placed = (
        P(("pb", "ka"), None),
        P(("pb", "ka"), None),
        P(None, ("pb", "ka")),
        P(None, ("pb", "ka")),
        P("pb"),
        P(("ka", "pb"), None),
        P(("ka", "pb"), None),
        P(("ka", "pb")),
        P(("ka", "pb")),
        P("ka"),
    )
    return jax.shard_map(
        local,
        mesh=mesh,
        in_specs=placed,
        out_specs=(P(("pb", "ka"), None), P(("ka", "pb"), None), P(("ka", "pb"), None)),
        check_vma=False,
    )
```

```python
import math

import jax
import jax.numpy as jnp
from jax import lax
from jax.experimental import pallas as pl
from jax.experimental.pallas import tpu as pltpu
from jax.sharding import PartitionSpec as P

HEADS = 8
HEAD_DIM = 128
SCALE = 1.0 / math.sqrt(HEAD_DIM)
LOG2E = math.log2(math.e)
MESH = pl.DeviceIdType.MESH
BF16 = jnp.bfloat16
FAR = 1 << 15
F32 = jnp.float32

TILES = (
    ((0, 0, 0), (1, 0, 0), (3, 0, 0), (0, 1, 0)),
    ((0, 0, 1), (1, 0, 1), (3, 0, 1), (0, 1, 1)),
    ((2, 0, 0), (1, 1, 0), (3, 1, 0), (2, 1, 0)),
    ((2, 0, 1), (1, 1, 1), (3, 1, 1), (2, 1, 1)),
)
CHUNKS = (((0, 0), (0, 1)), ((1, 0), (3, 0)), ((1, 1), (3, 1)), ((2, 0), (2, 1)))
STEPS = (
    (0, 0), (0, 1), (1, 1), (2, 0), (2, 1), (2, 2), (3, 0), (2, 3),
    (3, 1), (3, 3), (3, 2), (0, 3), (1, 3), (0, 2), (1, 2), (1, 0),
)
CROSS = 14
HAND_OVER = {(2, 0): 3, (1, 1): 4, (3, 1): 4, (2, 1): 5}
OFFSETS = tuple((d, dz) for dz in (0, 1) for d in (0, 1, 3, 2))
AWAY = OFFSETS[1:]
N_MESSAGES = 66


def place(groups, piece):
    for i, group in enumerate(groups):
        if piece in group:
            return i, group.index(piece)


def last_step(column, index):
    return max(i for i, step in enumerate(STEPS) if step[column] == index)


def dot(a, b, ca, cb):
    return lax.dot_general(a, b, (((ca,), (cb,)), ((), ())), preferred_element_type=F32)


def pick(table, s):
    value = jnp.int32(table[0])
    for i, entry in enumerate(table[1:], 1):
        value = jnp.where(s == i, jnp.int32(entry), value)
    return value


def flip(bit, by):
    return bit + by - 2 * bit * by


def kernel(
    q_hbm,
    o_hbm,
    log_ref,
    delta_ref,
    qstart_ref,
    kcode_ref,
    vcode_ref,
    kscale_ref,
    vscale_ref,
    kstart_ref,
    gq_ref,
    gk_ref,
    gv_ref,
    qo,
    ld,
    kv,
    dq_acc,
    dk_acc,
    dv_acc,
    p_t,
    ds_t,
    diff,
    dq_swap,
    dq_swapped,
    dq_out,
    dq_in,
    dkv_out,
    dkv_in,
    send_sems,
    recv_sems,
    local_sems,
):
    g = lax.axis_index("pb")
    k = lax.axis_index("ka")
    zh, y = g // 4, g % 4
    zl, x, core = k // 8, (k // 2) % 4, k % 2

    def query_owner(dx, dz, dc=0):
        return flip(zl, dz) * 8 + ((x + dx) % 4) * 2 + flip(core, dc)

    def key_owner(dy, dz):
        return flip(zh, dz) * 4 + (y + dy) % 4

    sibling = (g, query_owner(0, 0, 1))
    query_peer = {piece: (g, query_owner(*piece)) for piece in AWAY if 0 in piece}
    key_peer = {piece: (key_owner(*piece), k) for piece in AWAY if 0 in piece}
    peers = [sibling, *query_peer.values(), *key_peer.values()]
    barrier = pltpu.get_barrier_semaphore()
    for to in peers:
        pl.semaphore_signal(barrier, inc=1, device_id=to, device_id_type=MESH)

    messages, sent = {}, []

    def message(name, src, dst, to):
        i = len(messages)
        assert name not in messages and i < N_MESSAGES
        messages[name] = lambda: pltpu.make_async_remote_copy(
            src_ref=src,
            dst_ref=dst,
            send_sem=send_sems.at[i],
            recv_sem=recv_sems.at[i],
            device_id=to,
            device_id_type=MESH,
        )

    def send(*names):
        for name in names:
            sent.append(name)
            messages[name]().start()

    def arrived(*names):
        for name in names:
            messages[name]().wait_recv()

    def query_slot(piece, dc=0):
        tile, at = place(TILES, (*piece, dc))
        return tile * 4 + at

    def key_slot(piece):
        chunk, at = place(CHUNKS, piece)
        return chunk * 2 + at

    def back(piece):
        return (-piece[0]) % 4, piece[1]

    here = (0, 0)
    for dx in (1, 3, 2):
        for dz in (0, 1):
            to = query_peer[dx, 0]
            message(f"q{dx}{dz}", qo.at[query_slot((0, dz))], qo.at[query_slot(back((dx, dz)))], to)
            message(f"l{dx}{dz}", ld.at[query_slot((0, dz))], ld.at[query_slot(back((dx, dz)))], to)
            message(f"k{dx}{dz}", kv.at[key_slot((0, dz))], kv.at[key_slot(back((dx, dz)))], key_peer[dx, 0])
    message("q01", qo.at[query_slot(here)], qo.at[query_slot((0, 1))], query_peer[0, 1])
    message("l01", ld.at[query_slot(here)], ld.at[query_slot((0, 1))], query_peer[0, 1])
    message("k01", kv.at[key_slot(here)], kv.at[key_slot((0, 1))], key_peer[0, 1])
    for piece in OFFSETS:
        dx, dz = piece
        message(f"hq{dx}{dz}", qo.at[query_slot(piece)], qo.at[query_slot(piece, 1)], sibling)
        message(f"hl{dx}{dz}", ld.at[query_slot(piece)], ld.at[query_slot(piece, 1)], sibling)
        i = OFFSETS.index(piece)
        message(f"sq{dx}{dz}", dq_swap.at[i], dq_swapped.at[i], sibling)
    for i, piece in enumerate(AWAY):
        message(f"dq{piece[0]}{piece[1]}", dq_out.at[i], dq_in.at[i], query_peer[piece if piece == (0, 1) else (piece[0], 0)])
        message(f"dk{piece[0]}{piece[1]}", dkv_out.at[i], dkv_in.at[i], key_peer[piece if piece == (0, 1) else (piece[0], 0)])

    local = [
        pltpu.make_async_copy(q_hbm, qo.at[0, 0], local_sems.at[0]),
        pltpu.make_async_copy(o_hbm, qo.at[0, 1], local_sems.at[1]),
    ]
    for copy in local:
        copy.start()
    ld[0, 0:1, :] = jnp.concatenate([log_ref[h : h + 1, :] for h in range(HEADS)], axis=1) * LOG2E
    ld[0, 1:2, :] = jnp.concatenate([delta_ref[h : h + 1, :] for h in range(HEADS)], axis=1)
    ld[0, 2:8, :] = jnp.zeros((6, 256), F32)
    for i, (codes, factors) in enumerate(((kcode_ref, kscale_ref), (vcode_ref, vscale_ref))):
        for half in (0, 1):
            rows = pl.ds(half * 128, 128)
            factor = jnp.broadcast_to(factors[half : half + 1, :], (128, 128)).T
            kv[0, i, rows, :] = (codes[rows, :].astype(F32) * factor).astype(BF16)
    for copy in local:
        copy.wait()
    pl.semaphore_wait(barrier, len(peers))

    def came(letters, piece):
        dx, dz = back(piece)
        arrived(*(f"{letter}{dx}{dz}" for letter in letters))

    have = set()

    def need(letters, piece):
        name = f"{letters[0]}{piece[0]}{piece[1]}"
        if piece != here and name not in have:
            have.add(name)
            came(letters, piece)

    def hand_over(piece):
        need("ql", piece)
        send(f"hq{piece[0]}{piece[1]}", f"hl{piece[0]}{piece[1]}")

    send("k01", "q01", "l01", "k10", "k30", "q10", "l10", "q30", "l30", "hq00", "hl00", "k20", "q20", "l20")
    steps_apart = lax.broadcasted_iota(jnp.int32, (128, 256), 0) - lax.broadcasted_iota(jnp.int32, (128, 256), 1) % 32
    diff[...] = (steps_apart * FAR).astype(F32)
    dq_acc[...] = jnp.zeros_like(dq_acc)
    dk_acc[...] = jnp.zeros_like(dk_acc)
    dv_acc[...] = jnp.zeros_like(dv_acc)
    hand_over((0, 1))
    send("q11", "l11", "q31", "l31", "q21", "l21")
    hand_over((1, 0))
    hand_over((3, 0))
    need("k", (0, 1))
    send("k11", "k31", "k21")

    def ready(step):
        for piece, at in HAND_OVER.items():
            if at == step:
                hand_over(piece)
        chunk, tile = STEPS[step]
        if all(before[0] != chunk for before in STEPS[:step]):
            for piece in CHUNKS[chunk]:
                need("k", piece)
        if all(before[1] != tile for before in STEPS[:step]):
            for dx, dz, dc in TILES[tile]:
                if dc:
                    arrived(f"hq{dx}{dz}", f"hl{dx}{dz}")
                else:
                    need("ql", (dx, dz))

    def query_part(piece, dc=0):
        tile, at = place(TILES, (*piece, dc))
        return dq_acc[tile, :, at * 256 : (at + 1) * 256]

    def query_sum(piece):
        arrived(f"sq{piece[0]}{piece[1]}")
        return query_part(piece) + dq_swapped[OFFSETS.index(piece)].astype(F32)

    def swaps(step):
        return [(dx, dz) for dx, dz, dc in TILES[STEPS[step][1]] if dc and last_step(1, STEPS[step][1]) == step]

    def sums(step):
        for piece in AWAY:
            first, second = (last_step(1, place(TILES, (*piece, dc))[0]) for dc in (0, 1))
            at = max(first, second + 1)
            if at == step:
                yield piece

    def key_part(acc, piece):
        chunk, at = place(CHUNKS, piece)
        return acc[chunk, at * 256 : (at + 1) * 256]

    def key_sums(piece, others):
        total = [key_part(dk_acc, piece), key_part(dv_acc, piece)]
        for other in others:
            arrived(f"dk{other[0]}{other[1]}")
            total = [part + dkv_in[AWAY.index(other), n].astype(F32) for n, part in enumerate(total)]
        return total

    def done(step):
        for chunk in range(4):
            if last_step(0, chunk) == step:
                pieces = [piece for piece in CHUNKS[chunk] if piece[0]]
                for piece in pieces:
                    for n, acc in enumerate((dk_acc, dv_acc)):
                        dkv_out[AWAY.index(piece), n] = key_part(acc, piece).astype(BF16)
                send(*(f"dk{piece[0]}{piece[1]}" for piece in reversed(pieces)))
        for piece in swaps(step):
            dq_swap[OFFSETS.index(piece)] = query_part(piece, 1).astype(BF16)
        send(*(f"sq{dx}{dz}" for dx, dz in swaps(step)))
        if step == CROSS:
            total = key_sums((0, 1), ((1, 1), (3, 1), (2, 1)))
            for n in (0, 1):
                dkv_out[AWAY.index((0, 1)), n] = total[n].astype(BF16)
            send("dk01")
        hand_in(step)

    def hand_in(step):
        ready_now = sorted(sums(step), key=lambda piece: (-piece[1], -(piece[0] % 2), piece))
        for piece in ready_now:
            if piece == (0, 1):
                continue
            dq_out[AWAY.index(piece)] = query_sum(piece).astype(BF16)
            send(f"dq{piece[0]}{piece[1]}")

    def one_step(s, carry):
        for step in range(len(STEPS)):
            pl.when(s == step)(lambda step=step: ready(step))
        c, t = pick([step[0] for step in STEPS], s), pick([step[1] for step in STEPS], s)
        keys = jnp.concatenate([kv[2 * c, 0], kv[2 * c + 1, 0]], axis=0)
        values = jnp.concatenate([kv[2 * c, 1], kv[2 * c + 1, 1]], axis=0)
        starts = []
        for at in (0, 1):
            owner = key_owner(pick([chunk[at][0] for chunk in CHUNKS], c), pick([chunk[at][1] for chunk in CHUNKS], c))
            starts += [kstart_ref[owner * 2], kstart_ref[owner * 2 + 1]]
        offset = diff[...]
        all_q, all_o = [], []
        for at in range(4):
            piece = t * 4 + at
            owner = query_owner(*(pick([tile[at][n] for tile in TILES], t) for n in range(3)))
            first = qstart_ref[owner // 4] + (owner % 4) * 32
            q_rows = jnp.concatenate([qo[piece, 0, :, h * 128 : (h + 1) * 128] for h in range(HEADS)], axis=0)
            o_rows = jnp.concatenate([qo[piece, 1, :, h * 128 : (h + 1) * 128] for h in range(HEADS)], axis=0)
            logs, deltas = ld[piece, 0:1, :], ld[piece, 1:2, :]
            scores = dot(keys, q_rows, 1, 1)
            dprobs = dot(values, o_rows, 1, 1)
            unseen = jnp.concatenate([jnp.minimum(((first - start) * FAR).astype(F32) - offset, 0.0) for start in starts], axis=0)
            attention = jnp.exp2(scores * (SCALE * LOG2E) - logs + unseen)
            columns = pl.ds(at * 256, 256)
            p_t[:, columns] = attention.astype(BF16)
            ds_t[:, columns] = (attention * (dprobs - deltas)).astype(BF16)
            all_q.append(q_rows)
            all_o.append(o_rows)
        dv_acc[c] += dot(p_t[...], jnp.concatenate(all_o, axis=0), 1, 0)
        dk_acc[c] += dot(ds_t[...], jnp.concatenate(all_q, axis=0), 1, 0)
        dq_acc[t] += dot(keys.T, ds_t[...], 1, 0)
        for step in range(len(STEPS)):
            pl.when(s == step)(lambda step=step: done(step))
        return carry

    lax.fori_loop(0, len(STEPS), one_step, 0)

    hand_in(len(STEPS))
    total = query_sum((0, 1))
    for piece in ((1, 1), (3, 1), (2, 1)):
        arrived(f"dq{piece[0]}{piece[1]}")
        total += dq_in[AWAY.index(piece)].astype(F32)
    dq_out[AWAY.index((0, 1))] = total.astype(BF16)
    send("dq01")
    keys, values = key_sums(here, ((2, 0), (1, 0), (3, 0), (0, 1)))
    gk_ref[...] = (keys * SCALE).astype(BF16)
    gv_ref[...] = values.astype(BF16)
    total = query_sum(here)
    for piece in ((1, 0), (3, 0), (2, 0), (0, 1)):
        arrived(f"dq{piece[0]}{piece[1]}")
        total += dq_in[AWAY.index(piece)].astype(F32)
    total = (total * SCALE).T
    for h in range(HEADS):
        gq_ref[:, h * 128 : (h + 1) * 128] = total[h * 32 : (h + 1) * 32].astype(BF16)
    assert sorted(sent) == sorted(messages), set(messages) ^ set(sent)
    for make in messages.values():
        make().wait_send()


def finish(*refs):
    for i in range(3):
        refs[3 + i][...] = refs[i][...]


def local(
    queries, d_out, log_sums, deltas, query_start, key_codes, value_codes, key_scale, value_scale, key_start
):
    vmem = pl.BlockSpec(memory_space=pltpu.VMEM)
    smem = pl.BlockSpec(memory_space=pltpu.SMEM)
    anywhere = pl.BlockSpec(memory_space=pl.ANY)
    piece = (128, 256)
    outs = (
        jax.ShapeDtypeStruct((32, 1024), BF16),
        jax.ShapeDtypeStruct((256, 128), BF16),
        jax.ShapeDtypeStruct((256, 128), BF16),
    )
    grads = pl.pallas_call(
        kernel,
        out_shape=outs,
        in_specs=[anywhere, anywhere, vmem, vmem, smem, vmem, vmem, vmem, vmem, smem],
        out_specs=[vmem, vmem, vmem],
        scratch_shapes=[
            pltpu.VMEM((16, 2, 32, 1024), BF16),
            pltpu.VMEM((16, 8, 256), F32),
            pltpu.VMEM((8, 2, 256, 128), BF16),
            pltpu.VMEM((4, 128, 1024), F32),
            pltpu.VMEM((4, 512, 128), F32),
            pltpu.VMEM((4, 512, 128), F32),
            pltpu.VMEM((512, 1024), BF16),
            pltpu.VMEM((512, 1024), BF16),
            pltpu.VMEM((128, 256), F32),
            pltpu.VMEM((8, *piece), BF16),
            pltpu.VMEM((8, *piece), BF16),
            pltpu.VMEM((7, *piece), BF16),
            pltpu.VMEM((7, *piece), BF16),
            pltpu.VMEM((7, 2, 256, 128), BF16),
            pltpu.VMEM((7, 2, 256, 128), BF16),
            pltpu.SemaphoreType.DMA((N_MESSAGES,)),
            pltpu.SemaphoreType.DMA((N_MESSAGES,)),
            pltpu.SemaphoreType.DMA((2,)),
        ],
        compiler_params=pltpu.CompilerParams(
            collective_id=0, has_side_effects=True, vmem_limit_bytes=60 << 20
        ),
        name="fused",
    )(
        queries,
        d_out,
        log_sums,
        deltas,
        query_start,
        key_codes,
        value_codes,
        key_scale.reshape(2, 128),
        value_scale.reshape(2, 128),
        key_start,
    )
    return pl.pallas_call(finish, out_shape=outs, in_specs=[vmem] * 3, out_specs=[vmem] * 3, name="finish")(*grads)


def solution(mesh):
    placed = (
        P(("pb", "ka"), None),
        P(("pb", "ka"), None),
        P(None, ("pb", "ka")),
        P(None, ("pb", "ka")),
        P("pb"),
        P(("ka", "pb"), None),
        P(("ka", "pb"), None),
        P(("ka", "pb")),
        P(("ka", "pb")),
        P("ka"),
    )
    return jax.shard_map(
        local,
        mesh=mesh,
        in_specs=placed,
        out_specs=(P(("pb", "ka"), None), P(("ka", "pb"), None), P(("ka", "pb"), None)),
        check_vma=False,
    )
```
